32 devices in a mesh: gx: 4 (over z), yz: 8 (over y, x, core).
Axes of the slice: x: 2, y: 2, z: 4, core: 2. Of those that a mesh axis runs over, the one named last changes fastest.
Arguments:
- fields: float32 [5, 64, 2048], P(None, 'gx', 'yz'), may hold values from -6 to 6
- ghost_target: int32 [4, 512], P('gx', 'yz'), may hold values from 0 to 4095, as said below
- ghost_owner: int32 [4, 512, 1], P('gx', 'yz'), may hold values from 0 to 7; in each aligned block of 64 rows (0 to 63, 64 to 127, ..., all dimensions but the last counted through in order) at most 32 rows name the same one
- source_x: int32 [4, 512], P('gx', 'yz'), may hold values from 0 to 12
- source_col: int32 [4, 512], P('gx', 'yz'), may hold values from 0 to 255
- image_weights: float32 [4, 4, 512], P(None, 'gx', 'yz'), may hold values from 0 to 0.5
- sensor_bins: int32 [64, 2048], P('gx', 'yz'), may hold values from 0 to 7
Outputs:
- derivative: float32 [5, 64, 2048], P(None, 'gx', 'yz')
- filtered: float32 [5, 64, 2048], P(None, 'gx', 'yz')
The draws below stay inside these ranges and needn't reach their ends.
Inputs may be any that keep to these rules, and one draw needn't show every extreme that they name: `ghost_target`: the 64 target cells of one device are distinct. `ghost_owner`: within the 64 entries of one device no owner is named more than 32 times.
All inputs are finite; a program needn't handle non-finite values.
Results may differ from the reference program's by a relative error of at most 0.00002.
Values sent between devices are 32-bit elements; how exact they have to be, the bound alone decides.
A program may use at most 64 MiB of HBM per device.

```python
import math
import jax
import jax.numpy as jnp
import numpy as np
from jax import lax

CX = 16
COLS = 256
NF = 5
GH = 64
CAP = 32
NX = 64
NY = 2048
N_GX = 4
N_YZ = 8


def draw_ghost_target(key, part):
    stride = CX * COLS // GH
    base = jnp.arange(N_YZ * GH, dtype=jnp.int32) % GH * stride
    jitter = jax.random.randint(key, (N_GX, N_YZ * GH), 0, stride, dtype=jnp.int32)
    return base[None, :] + jitter


def with_ends(values, own_key, smallest, top_value):
    dims = values.shape
    place = [jax.random.randint(jax.random.fold_in(own_key, axis), (), 0, dims[axis]) for axis in range(len(dims))]
    values = values.at[tuple(place)].set(smallest)
    longest = dims.index(max(dims))
    place[longest] = (place[longest] + 1) % dims[longest]
    return values.at[tuple(place)].set(top_value)


def block_scale(stream_key, shape, shards, low, top_value):
    level = 1.0
    for position, shards_of in shards:
        draws = jax.random.uniform(jax.random.fold_in(jax.random.fold_in(stream_key, 6), position), (shards_of,), jnp.float32, low / len(shards), top_value / len(shards))
        level = level * jnp.repeat(jnp.exp(draws), shape[position] // shards_of).reshape((-1,) + (1,) * (len(shape) - 1 - position))
    return level


def deal_out(rng, own, number, rows, number_of, top, most, skew):
    ranking = jax.random.permutation(rng, number_of)
    crowded, ordinary = portions_of(number_of, rows * top, most, skew, True), portions_of(number_of, rows * top, most, skew, False)
    places = jnp.arange(number_of)

    def named(tallies, offset_by):
        used = int((tallies > 0).sum())
        fixed = max(1, used // 4)
        moved = fixed + (places - fixed + offset_by * (used - fixed)) % max(1, number_of - fixed)
        return jnp.zeros((number_of,), jnp.int32).at[ranking[jnp.where(places < fixed, places, moved)]].set(jnp.asarray(tallies, jnp.int32))

    tallies = jnp.where(number % 4 == 0, named(crowded, number // 4), named(ordinary, number - number // 4 - 1))
    mixed = jax.random.permutation(jax.random.fold_in(own, 3), number_of)
    donor, taker = mixed[0:number_of // 2 * 2:2], mixed[1:number_of // 2 * 2:2]
    slack = jnp.minimum(tallies[donor] - 1, most - tallies[taker]) // 2
    slack = jnp.where((donor == ranking[0]) | (taker == ranking[0]) | (tallies[taker] == 0), 0, jnp.maximum(slack, 0))
    moved = jax.random.randint(jax.random.fold_in(own, 4), (number_of // 2,), 0, 1 << 20) % (slack + 1)
    tallies = tallies.at[donor].add(-moved).at[taker].add(moved)
    items = jnp.searchsorted(jnp.cumsum(tallies), jnp.arange(rows * top), side="right").astype(jnp.int32)
    listing = items.reshape(top, rows).T
    listing = listing[jax.random.permutation(jax.random.fold_in(own, 1), rows)]
    offset_by = jax.random.randint(jax.random.fold_in(own, 2), (rows, 1), 0, top)
    return jnp.take_along_axis(listing, (jnp.arange(top)[None, :] + offset_by) % top, axis=1)


def portions_of(count, total, limit, lean, full):
    weights = [(1 << 20) // math.isqrt(standing ** lean) + 1 for standing in range(1, count + 1)]
    largest = limit if full else min(limit, max(-(-total // count), total * weights[0] // sum(weights)))
    least = 1 if total - largest >= count - 1 else 0
    given, surplus = [largest] + [least] * (count - 1), total - largest - least * (count - 1)
    while surplus > 0:
        movable = [i for i in range(1, count) if given[i] < largest] or [i for i in range(1, count) if given[i] < limit]
        whole, remaining = sum([weights[i] for i in movable]), surplus
        for i in movable:
            addition = min(limit - given[i], max(1, remaining * weights[i] // whole), surplus)
            given[i] = given[i] + addition
            surplus = surplus - addition
    return np.array(given)


def noise(stream_key, shape, deviation, bound, split=(), held_as=jnp.bfloat16):
    result = jax.random.normal(stream_key, shape, jnp.float32) * deviation
    if len(split) > 0:
        result = block_scale(stream_key, shape, split, -0.22, 0.18) * result
    return jnp.clip(result, min=-bound, max=bound).astype(held_as)


def setup_inputs(seed: int = 0) -> dict:
    streams_of = jax.random.split(jax.random.key(seed), 8)
    fields = noise(streams_of[0], (NF, NX, NY), 1.0, 6.0, ((1, 4), (2, 8)), jnp.float32)
    ghost_target = draw_ghost_target(jax.random.fold_in(streams_of[7], 71), 0)
    ghost_owner_keys = jax.random.split(jax.random.fold_in(streams_of[2], 1), N_GX * (N_YZ * GH) // GH)
    ghost_owner_turns = jax.random.permutation(jax.random.fold_in(streams_of[2], 3), N_GX * (N_YZ * GH) // GH)
    ghost_owner = jax.vmap(lambda own, number: deal_out(jax.random.fold_in(streams_of[2], 2), own, number, GH, N_YZ, 1, CAP, 2))(ghost_owner_keys, ghost_owner_turns).reshape((N_GX, N_YZ * GH, 1))
    source_x = with_ends(jax.random.randint(streams_of[3], (N_GX, N_YZ * GH), 0, CX - 3), jax.random.fold_in(streams_of[3], 1), 0, (CX - 3) - 1).astype(jnp.int32)
    source_col = with_ends(jax.random.randint(streams_of[4], (N_GX, N_YZ * GH), 0, COLS), jax.random.fold_in(streams_of[4], 1), 0, COLS - 1).astype(jnp.int32)
    image_weights = jnp.clip(0.5 * jax.random.uniform(streams_of[5], (4, N_GX, N_YZ * GH), jnp.float32) ** block_scale(streams_of[5], (4, N_GX, N_YZ * GH), ((1, 4), (2, 8)), -0.2, 0.2), 0.0, 0.5)
    sensor_bins = with_ends(jax.random.randint(streams_of[6], (NX, NY), 0, 8), jax.random.fold_in(streams_of[6], 1), 0, 7).astype(jnp.int32)
    return dict(fields=fields, ghost_target=ghost_target, ghost_owner=ghost_owner, source_x=source_x, source_col=source_col, image_weights=image_weights, sensor_bins=sensor_bins)


SIGNS = (1.0, -1.0, 1.0, 1.0, 1.0)
ALPHA_TOP = 0.499
ALPHA_STEP = 0.006

def filter_weights(alpha):
    twice = 2.0 * alpha - 1.0
    return ((193.0 + 126.0 * alpha) / 256.0, (105.0 + 302.0 * alpha) / 256.0, 15.0 * twice / 64.0, -45.0 * twice / 512.0, 5.0 * twice / 256.0, -twice / 512.0)

def stencils(padded, alpha, length):

    def plane(offset):
        return lax.slice_in_dim(padded, 5 + offset, 5 + offset + length, axis=1)
    slope = 7.0 / 9.0 * (plane(1) - plane(-1)) + 1.0 / 36.0 * (plane(2) - plane(-2))
    weights = filter_weights(alpha)
    smooth = weights[0] * plane(0)
    for offset in range(1, 6):
        smooth = smooth + 0.5 * weights[offset] * (plane(offset) + plane(-offset))
    return (slope, smooth)

def solve_rows(coupling, right):
    lower = coupling.at[..., 0].set(0.0)
    upper = coupling.at[..., -1].set(0.0)
    return lax.linalg.tridiagonal_solve(lower, jnp.ones_like(coupling), upper, right)

def solve_axis(coupling, right):
    moved = jnp.swapaxes(right, 1, 2)[..., None]
    link = jnp.swapaxes(coupling, 1, 2)
    return jnp.swapaxes(solve_rows(link, moved)[..., 0], 1, 2)

def reference(fields, ghost_target, ghost_owner, source_x, source_col, image_weights, sensor_bins):
    rows = jnp.arange(N_GX, dtype=jnp.int32)[:, None]
    block = (jnp.arange(N_YZ * GH, dtype=jnp.int32) // GH)[None, :]
    target_x = rows * CX + ghost_target // COLS
    target_y = block * COLS + ghost_target % COLS
    owner = ghost_owner[..., 0]
    start_x = rows * CX + source_x
    start_y = owner * COLS + source_col
    values = jnp.zeros((NF, N_GX, N_YZ * GH), jnp.float32)
    for offset in range(4):
        values = values + image_weights[offset][None] * fields[:, start_x + offset, start_y]
    values = values * jnp.array(SIGNS, jnp.float32)[:, None, None]
    filled = fields.at[:, target_x, target_y].set(values)
    padded = jnp.pad(filled, ((0, 0), (5, 5), (0, 0)))
    alpha = ALPHA_TOP - ALPHA_STEP * sensor_bins.astype(jnp.float32)
    slope, smooth = stencils(padded, alpha, NX)
    derivative = solve_axis(jnp.full(slope.shape, 1.0 / 3.0, jnp.float32), slope)
    filtered = solve_axis(jnp.broadcast_to(alpha, smooth.shape), smooth)
    return (derivative, filtered)
```

```python
import functools

import jax
import jax.numpy as jnp
from jax import lax
from jax.experimental import pallas as pl
from jax.experimental.pallas import tpu as pltpu
from jax.sharding import PartitionSpec as P

MESH = pl.DeviceIdType.MESH
SIGNS = (1.0, -1.0, 1.0, 1.0, 1.0)
ALPHA_TOP = 0.499
ALPHA_STEP = 0.006
HALO = 5
ROWS = 8


def thirds_factors(cells):
    a = 1.0 / 3.0
    link, inverse, last = ([], [], 0.0)
    for x in range(cells):
        inv = 1.0 / (1.0 - (a * last if x else 0.0))
        last = a * inv
        inverse.append(inv)
        link.append(last)
    left, right = ([0.0] * cells, [0.0] * cells)
    y = -link[0]
    left[0] = y
    for x in range(1, cells):
        y = -link[x] * y
        left[x] = y
    right[-1] = -link[-1]
    for x in range(cells - 2, -1, -1):
        left[x] = left[x] - link[x] * left[x + 1]
        right[x] = -link[x] * right[x + 1]
    return (link, inverse, left, right)


def thirds_interface(ranks, left, right):
    l0, l1, r0, r1 = (left[0], left[-1], right[0], right[-1])
    gain, out = (0.0, [])
    for q in range(ranks):
        s = 1.0 / (1.0 - l0 * gain)
        gf = r0 * s
        ng = r1 + l1 * gain * gf
        out.append((s, l0 * s, gf, l1, l1 * gain, ng))
        gain = ng
    return out


def split3(v):
    hi = v.astype(jnp.bfloat16)
    rest = v - hi.astype(jnp.float32)
    mid = rest.astype(jnp.bfloat16)
    low = (rest - mid.astype(jnp.float32)).astype(jnp.bfloat16)
    return (hi, mid, low)


def kernel(
    n_gx,
    n_yz,
    fields,
    target,
    owner,
    sx,
    col,
    weights,
    sensor,
    out_d,
    out_g,
    parts,
    onehot_t,
    reqs,
    reps,
    answers,
    fb,
    coef,
    gains,
    edges,
    unit_d,
    unit_g,
    sol,
    pick,
    req_s,
    req_r,
    rep_s,
    rep_r,
    gain_s,
    gain_r,
    halo_s,
    halo_r,
    edge_s,
    edge_r,
):
    F, X, C = fields.shape
    G = target.shape[1]
    GP = reqs.shape[2]
    pack = GP // G
    p = lax.axis_index("gx")
    r = lax.axis_index("yz")
    f32, bf16 = (jnp.float32, jnp.bfloat16)

    def yz(k):
        return (p, lax.rem(r + k + n_yz, n_yz))

    def gx(k):
        return (lax.rem(p + k + n_gx, n_gx), r)

    barrier = pltpu.get_barrier_semaphore()
    fb[...] = jnp.zeros_like(fb)
    edges[...] = jnp.zeros_like(edges)
    for k in range(1, n_yz):
        pl.semaphore_signal(barrier, inc=1, device_id=yz(k), device_id_type=MESH)
    for k in range(1, n_gx):
        pl.semaphore_signal(barrier, inc=1, device_id=gx(k), device_id_type=MESH)

    reqs[0] = jnp.zeros((ROWS, GP), f32)
    reqs[0, 0:1, 0:G] = col[...].astype(f32)
    reqs[0, 1:2, 0:G] = sx[...].astype(f32)
    reqs[0, 2:3, 0:G] = owner[...].astype(f32)
    for k in range(4):
        reqs[0, 3 + k : 4 + k, 0:G] = weights[k]

    pl.semaphore_wait(barrier, n_yz - 1 + n_gx - 1)

    def req_copy(k):
        return pltpu.make_async_remote_copy(
            src_ref=reqs.at[0],
            dst_ref=reqs.at[k],
            send_sem=req_s.at[k],
            recv_sem=req_r.at[k],
            device_id=yz(k),
            device_id_type=MESH,
        )

    for k in range(1, n_yz):
        req_copy(k).start()

    link = []
    inverse = []
    for x in range(X):
        b = jnp.broadcast_to(sensor[x : x + 1, :].astype(f32), (ROWS, C))
        alpha = ALPHA_TOP - ALPHA_STEP * b
        den = jnp.ones((ROWS, C), f32) if x == 0 else 1.0 - alpha * link[-1]
        inv = 1.0 / den
        link.append(alpha * inv)
        inverse.append(inv)
        twice = 2.0 * alpha - 1.0
        coef[0, x] = inv * ((193.0 + 126.0 * alpha) / 256.0)
        coef[1, x] = inv * ((105.0 + 302.0 * alpha) / 512.0)
        scaled = inv * twice
        coef[2, x] = scaled * (15.0 / 128.0)
        coef[3, x] = scaled * (-45.0 / 1024.0)
        coef[4, x] = scaled * (5.0 / 512.0)
        coef[5, x] = scaled * (-1.0 / 1024.0)
        coef[6, x] = link[-1]
    y = [-link[0]]
    for x in range(1, X):
        y.append(-link[x] * y[-1])
    ul, ur = (y[-1], -link[-1])
    unit_g[0, X - 1 : X, :] = ul[0:1, :]
    unit_g[1, X - 1 : X, :] = ur[0:1, :]
    ends = [None, ul, None, ur]
    for x in range(X - 2, -1, -1):
        ul = y[x] - link[x] * ul
        ur = -link[x] * ur
        unit_g[0, x : x + 1, :] = ul[0:1, :]
        unit_g[1, x : x + 1, :] = ur[0:1, :]
    ends[0], ends[2] = (ul, ur)
    mine = gains.at[p]
    for i in range(4):
        mine[2 * i : 2 * i + 2, :] = ends[i][0:2, :]

    def gain_copy(k):
        return pltpu.make_async_remote_copy(
            src_ref=gains.at[p],
            dst_ref=gains.at[p],
            send_sem=gain_s.at[k],
            recv_sem=gain_r.at[k],
            device_id=gx(k),
            device_id_type=MESH,
        )

    for k in range(1, n_gx):
        gain_copy(k).start()

    flat = fields[...].reshape(F * X, C)
    for i, piece in enumerate(split3(flat)):
        parts[i * F * X : (i + 1) * F * X, :] = piece

    lane_c = lax.broadcasted_iota(jnp.int32, (C, GP), 0)
    row_x = lax.broadcasted_iota(jnp.int32, (X, GP), 0)
    own = r.astype(f32)

    def rep_copy(k):
        return pltpu.make_async_remote_copy(
            src_ref=answers.at[k // pack],
            dst_ref=reps.at[k],
            send_sem=rep_s.at[k],
            recv_sem=rep_r.at[k],
            device_id=yz(-k),
            device_id_type=MESH,
        )

    for j in range(n_yz // pack):
        block = None
        for i in range(pack):
            k = j * pack + i
            if k:
                req_copy(k).wait_recv()
            piece = reqs[k]
            if i:
                piece = pltpu.roll(piece, i * G, 1)
            block = piece if block is None else block + piece
        hot = jnp.where(lane_c == block[0:1, :].astype(jnp.int32), 1.0, 0.0).astype(bf16)
        got = jnp.dot(parts[...], hot, preferred_element_type=f32)
        offset = row_x - block[1:2, :].astype(jnp.int32)
        mask = jnp.zeros((X, GP), f32)
        for k in range(4):
            mask = jnp.where(offset == k, block[3 + k : 4 + k, :], mask)
        mask = jnp.where(block[2:3, :] == own, mask, 0.0)
        n = F * X
        total = got[0:n] + got[n : 2 * n] + got[2 * n : 3 * n]
        rows = []
        for f in range(F):
            value = jnp.sum(total[f * X : (f + 1) * X] * mask, axis=0, keepdims=True)
            rows.append(SIGNS[f] * value)
        rows.append(jnp.zeros((ROWS - F, GP), f32))
        answers[j] = jnp.concatenate(rows, axis=0)
        for i in range(pack):
            k = j * pack + i
            if k:
                rep_copy(k).start()

    bits = C.bit_length() - 1
    goal = target[...]
    lane = lax.broadcasted_iota(jnp.int32, (1, G), 1)
    goal_x = jnp.right_shift(goal, bits)
    goal_c = jnp.bitwise_and(goal, C - 1)
    wide = lax.broadcasted_iota(jnp.int32, (C, G), 0)
    hit = jnp.where(wide == goal_c, 1.0, 0.0)
    if GP > G:
        hit = jnp.concatenate([hit, jnp.zeros((C, GP - G), f32)], axis=1)
        goal_x = jnp.concatenate([goal_x, jnp.full((1, GP - G), -1, jnp.int32)], axis=1)
    hit = hit.T.astype(bf16)
    for i in range(3):
        onehot_t[i * GP : (i + 1) * GP, :] = hit
    goal_x = jnp.broadcast_to(goal_x, (ROWS, GP))
    ones = jnp.concatenate([jnp.where(goal_x == x, 1.0, 0.0) for x in range(X)], axis=0)
    taken = jnp.dot(ones.astype(bf16), hit, preferred_element_type=f32)
    for x in range(X):
        for f in range(F):
            fb[HALO + x, f : f + 1, :] = fields[f, x : x + 1, :]
    for x in range(X):
        here = taken[x * ROWS : (x + 1) * ROWS]
        fb[HALO + x] = jnp.where(here > 0.5, 0.0, fb[HALO + x])

    link_d, inverse_d, left_d, right_d = thirds_factors(X)
    inter_d = thirds_interface(n_gx, left_d, right_d)
    for x in range(X):
        unit_d[0, x : x + 1, :] = jnp.full((1, C), left_d[x], f32)
        unit_d[1, x : x + 1, :] = jnp.full((1, C), right_d[x], f32)

    inter_g = []
    gain = jnp.zeros((1, C), f32)
    for k in range(1, n_gx):
        gain_from(gains, gain_s, gain_r, k, p, r, n_gx).wait_recv()
    for q in range(n_gx):
        l0, l1 = (gains[q, 0:1, :], gains[q, 2:3, :])
        r0, r1 = (gains[q, 4:5, :], gains[q, 6:7, :])
        s = 1.0 / (1.0 - l0 * gain)
        gf = r0 * s
        ng = r1 + l1 * gain * gf
        inter_g.append((s, l0 * s, gf, l1, l1 * gain, ng))
        gain = ng

    total = answers[0]
    side = None
    for k in range(1, n_yz):
        rep_copy(k).wait_recv()
    sums = [answers[0]] + [None] * (pack - 1)
    for k in range(1, n_yz):
        i = k % pack
        sums[i] = reps[k] if sums[i] is None else sums[i] + reps[k]
    total = sums[0]
    for i in range(1, pack):
        total = total + pltpu.roll(sums[i], GP - i * G, 1)
    stack = []
    for piece in split3(total):
        wide_piece = piece.astype(f32)
        stack.append(
            jnp.concatenate([jnp.where(goal_x == x, wide_piece, 0.0) for x in range(X)], axis=0)
        )
    spread = jnp.dot(
        jnp.concatenate(stack, axis=1).astype(bf16), onehot_t[...], preferred_element_type=f32
    )
    for x in range(X):
        fb[HALO + x] = fb[HALO + x] + spread[x * ROWS : (x + 1) * ROWS]

    def to_above():
        return pltpu.make_async_remote_copy(
            src_ref=fb.at[pl.ds(X, HALO)],
            dst_ref=fb.at[pl.ds(0, HALO)],
            send_sem=halo_s.at[0],
            recv_sem=halo_r.at[0],
            device_id=gx(1),
            device_id_type=MESH,
        )

    def to_below():
        return pltpu.make_async_remote_copy(
            src_ref=fb.at[pl.ds(HALO, HALO)],
            dst_ref=fb.at[pl.ds(HALO + X, HALO)],
            send_sem=halo_s.at[1],
            recv_sem=halo_r.at[1],
            device_id=gx(-1),
            device_id_type=MESH,
        )

    @pl.when(p < n_gx - 1)
    def _():
        to_above().start()

    @pl.when(p > 0)
    def _():
        to_below().start()

    @pl.when(p > 0)
    def _():
        to_above().wait_recv()

    @pl.when(p < n_gx - 1)
    def _():
        to_below().wait_recv()

    yd, yg = ([], [])
    for x in range(X):
        at = HALO + x
        near, next2 = (fb[at + 1], fb[at + 2])
        back, back2 = (fb[at - 1], fb[at - 2])
        slope = (7.0 / 9.0 * inverse_d[x]) * (near - back) + (1.0 / 36.0 * inverse_d[x]) * (
            next2 - back2
        )
        smooth = coef[0, x] * fb[at] + coef[1, x] * (near + back) + coef[2, x] * (next2 + back2)
        for n in range(3, 6):
            smooth = smooth + coef[n, x] * (fb[at + n] + fb[at - n])
        if x:
            slope = slope - link_d[x] * yd[-1]
            smooth = smooth - coef[6, x] * yg[-1]
        yd.append(slope)
        yg.append(smooth)
    ud, ug = (yd[-1], yg[-1])
    last_d, last_g = (ud, ug)
    sol[0, X - 1] = ud
    sol[1, X - 1] = ug
    for x in range(X - 2, -1, -1):
        ud = yd[x] - link_d[x] * ud
        ug = yg[x] - coef[6, x] * ug
        sol[0, x] = ud
        sol[1, x] = ug
    here = edges.at[p]
    for i, v in enumerate((ud, last_d, ug, last_g)):
        here[i * F : (i + 1) * F, :] = v[0:F]

    def edge_copy(k, rank, peer):
        return pltpu.make_async_remote_copy(
            src_ref=edges.at[rank],
            dst_ref=edges.at[rank],
            send_sem=edge_s.at[k],
            recv_sem=edge_r.at[k],
            device_id=peer,
            device_id_type=MESH,
        )

    for k in range(1, n_gx):
        edge_copy(k, p, gx(k)).start()

    for x in range(X):
        for f in range(F):
            out_d[f, x : x + 1, :] = sol[0, x, f : f + 1, :]
            out_g[f, x : x + 1, :] = sol[1, x, f : f + 1, :]

    for k in range(1, n_gx):
        edge_copy(k, lax.rem(p - k + n_gx, n_gx), gx(-k)).wait_recv()

    for which, inter in enumerate((inter_d, inter_g)):
        hold = jnp.zeros((F, C), f32)
        first = []
        pick[which, 0, 0:F, :] = hold
        pick[which, 1, 0:1, :] = jnp.zeros((1, C), f32)
        for q in range(n_gx):
            s, ls, gf, l1, lg, ng = inter[q]
            h0 = edges[q, which * 2 * F : which * 2 * F + F, :]
            h1 = edges[q, which * 2 * F + F : which * 2 * F + 2 * F, :]
            hf = s * h0 + ls * hold
            hold = h1 + l1 * hold + lg * hf
            first.append(hf)
            pick[which, 3 * (q + 1), 0:F, :] = hold
            pick[which, 3 * (q + 1) + 1, 0:1, :] = jnp.broadcast_to(jnp.asarray(ng, f32), (1, C))
        after = jnp.zeros((F, C), f32)
        pick[which, 3 * n_gx + 2, 0:F, :] = after
        for q in range(n_gx - 1, -1, -1):
            after = first[q] + inter[q][2] * after
            pick[which, 3 * q + 2, 0:F, :] = after
        own_first = pick[which, 3 * p + 2, 0:F, :]
        before = pick[which, 3 * p, 0:F, :] + pick[which, 3 * p + 1, 0:1, :] * own_first
        before = jnp.where(p > 0, before, 0.0)
        after = pick[which, 3 * (p + 1) + 2, 0:F, :]
        unit, out = ((unit_d, out_d), (unit_g, out_g))[which]
        lower, upper = (unit[0], unit[1])
        for f in range(F):
            out[f] = out[f] + before[f : f + 1, :] * lower + after[f : f + 1, :] * upper

    for k in range(1, n_yz):
        req_copy(k).wait_send()
        rep_copy(k).wait_send()
    for k in range(1, n_gx):
        gain_copy(k).wait_send()
        edge_copy(k, p, gx(k)).wait_send()

    @pl.when(p < n_gx - 1)
    def _():
        to_above().wait_send()

    @pl.when(p > 0)
    def _():
        to_below().wait_send()


def gain_from(gains, gain_s, gain_r, k, p, r, n_gx):
    rank = lax.rem(p - k + n_gx, n_gx)
    return pltpu.make_async_remote_copy(
        src_ref=gains.at[rank],
        dst_ref=gains.at[rank],
        send_sem=gain_s.at[k],
        recv_sem=gain_r.at[k],
        device_id=(rank, r),
        device_id_type=MESH,
    )


def shards(fields, target, owner, sx, col, weights, sensor):
    F, X, C = fields.shape
    G = target.shape[1]
    n_gx, n_yz = (lax.axis_size("gx"), lax.axis_size("yz"))
    GP = max(G, 128)
    pack = GP // G
    edge_rows = -(-4 * F // ROWS) * ROWS
    f32, bf16 = (jnp.float32, jnp.bfloat16)
    vmem = pl.BlockSpec(memory_space=pltpu.VMEM)
    dma = pltpu.SemaphoreType.DMA
    out = jax.ShapeDtypeStruct(fields.shape, f32)
    return pl.pallas_call(
        functools.partial(kernel, n_gx, n_yz),
        out_shape=(out, out),
        in_specs=[vmem] * 7,
        out_specs=(vmem, vmem),
        scratch_shapes=[
            pltpu.VMEM((3 * F * X, C), bf16),
            pltpu.VMEM((3 * GP, C), bf16),
            pltpu.VMEM((n_yz, ROWS, GP), f32),
            pltpu.VMEM((n_yz, ROWS, GP), f32),
            pltpu.VMEM((n_yz // pack, ROWS, GP), f32),
            pltpu.VMEM((X + 2 * HALO, ROWS, C), f32),
            pltpu.VMEM((7, X, ROWS, C), f32),
            pltpu.VMEM((n_gx, ROWS, C), f32),
            pltpu.VMEM((n_gx, edge_rows, C), f32),
            pltpu.VMEM((2, X, C), f32),
            pltpu.VMEM((2, X, C), f32),
            pltpu.VMEM((2, X, ROWS, C), f32),
            pltpu.VMEM((2, 3 * (n_gx + 1), ROWS, C), f32),
            dma((n_yz,)),
            dma((n_yz,)),
            dma((n_yz,)),
            dma((n_yz,)),
            dma((n_gx,)),
            dma((n_gx,)),
            dma((2,)),
            dma((2,)),
            dma((n_gx,)),
            dma((n_gx,)),
        ],
        compiler_params=pltpu.CompilerParams(collective_id=0, has_side_effects=True),
    )(fields, target, owner.reshape(target.shape), sx, col, weights, sensor)


def solution(mesh):
    placed = (
        P(None, "gx", "yz"),
        P("gx", "yz"),
        P("gx", "yz", None),
        P("gx", "yz"),
        P("gx", "yz"),
        P(None, "gx", "yz"),
        P("gx", "yz"),
    )
    return jax.shard_map(
        shards,
        mesh=mesh,
        in_specs=placed,
        out_specs=(P(None, "gx", "yz"), P(None, "gx", "yz")),
        check_vma=False,
    )
```

```python
import functools

import jax
import jax.numpy as jnp
from jax import lax
from jax.experimental import pallas as pl
from jax.experimental.pallas import tpu as pltpu
from jax.sharding import PartitionSpec as P

MESH = pl.DeviceIdType.MESH
SIGNS = (1.0, -1.0, 1.0, 1.0, 1.0)
ALPHA_TOP = 0.499
ALPHA_STEP = 0.006
HALO = 5
ROWS = 8


def thirds_factors(cells):
    a = 1.0 / 3.0
    link, inverse, last = ([], [], 0.0)
    for x in range(cells):
        inv = 1.0 / (1.0 - (a * last if x else 0.0))
        last = a * inv
        inverse.append(inv)
        link.append(last)
    left, right = ([0.0] * cells, [0.0] * cells)
    y = -link[0]
    left[0] = y
    for x in range(1, cells):
        y = -link[x] * y
        left[x] = y
    right[-1] = -link[-1]
    for x in range(cells - 2, -1, -1):
        left[x] = left[x] - link[x] * left[x + 1]
        right[x] = -link[x] * right[x + 1]
    return (link, inverse, left, right)


def thirds_interface(ranks, left, right):
    l0, l1, r0, r1 = (left[0], left[-1], right[0], right[-1])
    gain, out = (0.0, [])
    for q in range(ranks):
        s = 1.0 / (1.0 - l0 * gain)
        gf = r0 * s
        ng = r1 + l1 * gain * gf
        out.append((s, l0 * s, gf, l1, l1 * gain, ng))
        gain = ng
    return out


def split3(v):
    hi = v.astype(jnp.bfloat16)
    rest = v - hi.astype(jnp.float32)
    mid = rest.astype(jnp.bfloat16)
    low = (rest - mid.astype(jnp.float32)).astype(jnp.bfloat16)
    return (hi, mid, low)


def kernel(
    n_gx,
    n_yz,
    fields_hbm,
    target_hbm,
    owner_hbm,
    sx_hbm,
    col_hbm,
    weights_hbm,
    sensor_hbm,
    out_d,
    out_g,
    fields,
    target,
    owner,
    sx,
    col,
    weights,
    sensor,
    load_sem,
    parts,
    onehot_t,
    reqs,
    reps,
    answers,
    fb,
    coef,
    gains,
    edges,
    unit_d,
    unit_g,
    sol,
    pick,
    req_s,
    req_r,
    rep_s,
    rep_r,
    gain_s,
    gain_r,
    halo_s,
    halo_r,
    edge_s,
    edge_r,
):
    F, X, C = fields.shape
    G = target.shape[1]
    GP = reqs.shape[2]
    pack = GP // G
    p = lax.axis_index("gx")
    r = lax.axis_index("yz")
    f32, bf16 = (jnp.float32, jnp.bfloat16)

    def yz(k):
        return (p, lax.rem(r + k + n_yz, n_yz))

    def gx(k):
        return (lax.rem(p + k + n_gx, n_gx), r)

    barrier = pltpu.get_barrier_semaphore()
    loads = [
        pltpu.make_async_copy(src, dst, load_sem.at[i])
        for i, (src, dst) in enumerate(
            (
                (owner_hbm, owner),
                (sx_hbm, sx),
                (col_hbm, col),
                (weights_hbm, weights),
                (sensor_hbm, sensor),
                (target_hbm, target),
                (fields_hbm, fields),
            )
        )
    ]
    for copy in loads:
        copy.start()
    fb[...] = jnp.zeros_like(fb)
    edges[...] = jnp.zeros_like(edges)
    for k in range(1, n_yz):
        pl.semaphore_signal(barrier, inc=1, device_id=yz(k), device_id_type=MESH)
    for k in range(1, n_gx):
        pl.semaphore_signal(barrier, inc=1, device_id=gx(k), device_id_type=MESH)

    for copy in loads[:4]:
        copy.wait()
    reqs[0] = jnp.zeros((ROWS, GP), f32)
    reqs[0, 0:1, 0:G] = col[...].astype(f32)
    reqs[0, 1:2, 0:G] = sx[...].astype(f32)
    reqs[0, 2:3, 0:G] = owner[...].astype(f32)
    for k in range(4):
        reqs[0, 3 + k : 4 + k, 0:G] = weights[k]

    pl.semaphore_wait(barrier, n_yz - 1 + n_gx - 1)

    def req_copy(k):
        return pltpu.make_async_remote_copy(
            src_ref=reqs.at[0],
            dst_ref=reqs.at[k],
            send_sem=req_s.at[k],
            recv_sem=req_r.at[k],
            device_id=yz(k),
            device_id_type=MESH,
        )

    for k in range(1, n_yz):
        req_copy(k).start()

    for copy in loads[4:]:
        copy.wait()
    link = []
    inverse = []
    for x in range(X):
        b = jnp.broadcast_to(sensor[x : x + 1, :].astype(f32), (ROWS, C))
        alpha = ALPHA_TOP - ALPHA_STEP * b
        den = jnp.ones((ROWS, C), f32) if x == 0 else 1.0 - alpha * link[-1]
        inv = 1.0 / den
        link.append(alpha * inv)
        inverse.append(inv)
        twice = 2.0 * alpha - 1.0
        coef[0, x] = inv * ((193.0 + 126.0 * alpha) / 256.0)
        coef[1, x] = inv * ((105.0 + 302.0 * alpha) / 512.0)
        scaled = inv * twice
        coef[2, x] = scaled * (15.0 / 128.0)
        coef[3, x] = scaled * (-45.0 / 1024.0)
        coef[4, x] = scaled * (5.0 / 512.0)
        coef[5, x] = scaled * (-1.0 / 1024.0)
        coef[6, x] = link[-1]
    y = [-link[0]]
    for x in range(1, X):
        y.append(-link[x] * y[-1])
    ul, ur = (y[-1], -link[-1])
    unit_g[0, X - 1 : X, :] = ul[0:1, :]
    unit_g[1, X - 1 : X, :] = ur[0:1, :]
    ends = [None, ul, None, ur]
    for x in range(X - 2, -1, -1):
        ul = y[x] - link[x] * ul
        ur = -link[x] * ur
        unit_g[0, x : x + 1, :] = ul[0:1, :]
        unit_g[1, x : x + 1, :] = ur[0:1, :]
    ends[0], ends[2] = (ul, ur)
    mine = gains.at[p]
    for i in range(4):
        mine[2 * i : 2 * i + 2, :] = ends[i][0:2, :]

    def gain_copy(k):
        return pltpu.make_async_remote_copy(
            src_ref=gains.at[p],
            dst_ref=gains.at[p],
            send_sem=gain_s.at[k],
            recv_sem=gain_r.at[k],
            device_id=gx(k),
            device_id_type=MESH,
        )

    for k in range(1, n_gx):
        gain_copy(k).start()

    flat = fields[...].reshape(F * X, C)
    for i, piece in enumerate(split3(flat)):
        parts[i * F * X : (i + 1) * F * X, :] = piece

    lane_c = lax.broadcasted_iota(jnp.int32, (C, GP), 0)
    row_x = lax.broadcasted_iota(jnp.int32, (X, GP), 0)
    own = r.astype(f32)

    def rep_copy(k):
        return pltpu.make_async_remote_copy(
            src_ref=answers.at[k // pack],
            dst_ref=reps.at[k],
            send_sem=rep_s.at[k],
            recv_sem=rep_r.at[k],
            device_id=yz(-k),
            device_id_type=MESH,
        )

    for j in range(n_yz // pack):
        block = None
        for i in range(pack):
            k = j * pack + i
            if k:
                req_copy(k).wait_recv()
            piece = reqs[k]
            if i:
                piece = pltpu.roll(piece, i * G, 1)
            block = piece if block is None else block + piece
        hot = jnp.where(lane_c == block[0:1, :].astype(jnp.int32), 1.0, 0.0).astype(bf16)
        got = jnp.dot(parts[...], hot, preferred_element_type=f32)
        offset = row_x - block[1:2, :].astype(jnp.int32)
        mask = jnp.zeros((X, GP), f32)
        for k in range(4):
            mask = jnp.where(offset == k, block[3 + k : 4 + k, :], mask)
        mask = jnp.where(block[2:3, :] == own, mask, 0.0)
        n = F * X
        total = got[0:n] + got[n : 2 * n] + got[2 * n : 3 * n]
        rows = []
        for f in range(F):
            value = jnp.sum(total[f * X : (f + 1) * X] * mask, axis=0, keepdims=True)
            rows.append(SIGNS[f] * value)
        rows.append(jnp.zeros((ROWS - F, GP), f32))
        answers[j] = jnp.concatenate(rows, axis=0)
        for i in range(pack):
            k = j * pack + i
            if k:
                rep_copy(k).start()

    bits = C.bit_length() - 1
    goal = target[...]
    lane = lax.broadcasted_iota(jnp.int32, (1, G), 1)
    goal_x = jnp.right_shift(goal, bits)
    goal_c = jnp.bitwise_and(goal, C - 1)
    wide = lax.broadcasted_iota(jnp.int32, (C, G), 0)
    hit = jnp.where(wide == goal_c, 1.0, 0.0)
    if GP > G:
        hit = jnp.concatenate([hit, jnp.zeros((C, GP - G), f32)], axis=1)
        goal_x = jnp.concatenate([goal_x, jnp.full((1, GP - G), -1, jnp.int32)], axis=1)
    hit = hit.T.astype(bf16)
    for i in range(3):
        onehot_t[i * GP : (i + 1) * GP, :] = hit
    goal_x = jnp.broadcast_to(goal_x, (ROWS, GP))
    ones = jnp.concatenate([jnp.where(goal_x == x, 1.0, 0.0) for x in range(X)], axis=0)
    taken = jnp.dot(ones.astype(bf16), hit, preferred_element_type=f32)
    for x in range(X):
        for f in range(F):
            fb[HALO + x, f : f + 1, :] = fields[f, x : x + 1, :]
    for x in range(X):
        here = taken[x * ROWS : (x + 1) * ROWS]
        fb[HALO + x] = jnp.where(here > 0.5, 0.0, fb[HALO + x])

    link_d, inverse_d, left_d, right_d = thirds_factors(X)
    inter_d = thirds_interface(n_gx, left_d, right_d)
    for x in range(X):
        unit_d[0, x : x + 1, :] = jnp.full((1, C), left_d[x], f32)
        unit_d[1, x : x + 1, :] = jnp.full((1, C), right_d[x], f32)

    inter_g = []
    gain = jnp.zeros((1, C), f32)
    for k in range(1, n_gx):
        gain_from(gains, gain_s, gain_r, k, p, r, n_gx).wait_recv()
    for q in range(n_gx):
        l0, l1 = (gains[q, 0:1, :], gains[q, 2:3, :])
        r0, r1 = (gains[q, 4:5, :], gains[q, 6:7, :])
        s = 1.0 / (1.0 - l0 * gain)
        gf = r0 * s
        ng = r1 + l1 * gain * gf
        inter_g.append((s, l0 * s, gf, l1, l1 * gain, ng))
        gain = ng

    total = answers[0]
    side = None
    for k in range(1, n_yz):
        rep_copy(k).wait_recv()
    sums = [answers[0]] + [None] * (pack - 1)
    for k in range(1, n_yz):
        i = k % pack
        sums[i] = reps[k] if sums[i] is None else sums[i] + reps[k]
    total = sums[0]
    for i in range(1, pack):
        total = total + pltpu.roll(sums[i], GP - i * G, 1)
    stack = []
    for piece in split3(total):
        wide_piece = piece.astype(f32)
        stack.append(
            jnp.concatenate([jnp.where(goal_x == x, wide_piece, 0.0) for x in range(X)], axis=0)
        )
    spread = jnp.dot(
        jnp.concatenate(stack, axis=1).astype(bf16), onehot_t[...], preferred_element_type=f32
    )
    for x in range(X):
        fb[HALO + x] = fb[HALO + x] + spread[x * ROWS : (x + 1) * ROWS]

    def to_above():
        return pltpu.make_async_remote_copy(
            src_ref=fb.at[pl.ds(X, HALO)],
            dst_ref=fb.at[pl.ds(0, HALO)],
            send_sem=halo_s.at[0],
            recv_sem=halo_r.at[0],
            device_id=gx(1),
            device_id_type=MESH,
        )

    def to_below():
        return pltpu.make_async_remote_copy(
            src_ref=fb.at[pl.ds(HALO, HALO)],
            dst_ref=fb.at[pl.ds(HALO + X, HALO)],
            send_sem=halo_s.at[1],
            recv_sem=halo_r.at[1],
            device_id=gx(-1),
            device_id_type=MESH,
        )

    @pl.when(p < n_gx - 1)
    def _():
        to_above().start()

    @pl.when(p > 0)
    def _():
        to_below().start()

    @pl.when(p > 0)
    def _():
        to_above().wait_recv()

    @pl.when(p < n_gx - 1)
    def _():
        to_below().wait_recv()

    yd, yg = ([], [])
    for x in range(X):
        at = HALO + x
        near, next2 = (fb[at + 1], fb[at + 2])
        back, back2 = (fb[at - 1], fb[at - 2])
        slope = (7.0 / 9.0 * inverse_d[x]) * (near - back) + (1.0 / 36.0 * inverse_d[x]) * (
            next2 - back2
        )
        smooth = coef[0, x] * fb[at] + coef[1, x] * (near + back) + coef[2, x] * (next2 + back2)
        for n in range(3, 6):
            smooth = smooth + coef[n, x] * (fb[at + n] + fb[at - n])
        if x:
            slope = slope - link_d[x] * yd[-1]
            smooth = smooth - coef[6, x] * yg[-1]
        yd.append(slope)
        yg.append(smooth)
    ud, ug = (yd[-1], yg[-1])
    last_d, last_g = (ud, ug)
    sol[0, X - 1] = ud
    sol[1, X - 1] = ug
    for x in range(X - 2, -1, -1):
        ud = yd[x] - link_d[x] * ud
        ug = yg[x] - coef[6, x] * ug
        sol[0, x] = ud
        sol[1, x] = ug
    here = edges.at[p]
    for i, v in enumerate((ud, last_d, ug, last_g)):
        here[i * F : (i + 1) * F, :] = v[0:F]

    def edge_copy(k, rank, peer):
        return pltpu.make_async_remote_copy(
            src_ref=edges.at[rank],
            dst_ref=edges.at[rank],
            send_sem=edge_s.at[k],
            recv_sem=edge_r.at[k],
            device_id=peer,
            device_id_type=MESH,
        )

    for k in range(1, n_gx):
        edge_copy(k, p, gx(k)).start()

    for x in range(X):
        for f in range(F):
            out_d[f, x : x + 1, :] = sol[0, x, f : f + 1, :]
            out_g[f, x : x + 1, :] = sol[1, x, f : f + 1, :]

    for k in range(1, n_gx):
        edge_copy(k, lax.rem(p - k + n_gx, n_gx), gx(-k)).wait_recv()

    for which, inter in enumerate((inter_d, inter_g)):
        hold = jnp.zeros((F, C), f32)
        first = []
        pick[which, 0, 0:F, :] = hold
        pick[which, 1, 0:1, :] = jnp.zeros((1, C), f32)
        for q in range(n_gx):
            s, ls, gf, l1, lg, ng = inter[q]
            h0 = edges[q, which * 2 * F : which * 2 * F + F, :]
            h1 = edges[q, which * 2 * F + F : which * 2 * F + 2 * F, :]
            hf = s * h0 + ls * hold
            hold = h1 + l1 * hold + lg * hf
            first.append(hf)
            pick[which, 3 * (q + 1), 0:F, :] = hold
            pick[which, 3 * (q + 1) + 1, 0:1, :] = jnp.broadcast_to(jnp.asarray(ng, f32), (1, C))
        after = jnp.zeros((F, C), f32)
        pick[which, 3 * n_gx + 2, 0:F, :] = after
        for q in range(n_gx - 1, -1, -1):
            after = first[q] + inter[q][2] * after
            pick[which, 3 * q + 2, 0:F, :] = after
        own_first = pick[which, 3 * p + 2, 0:F, :]
        before = pick[which, 3 * p, 0:F, :] + pick[which, 3 * p + 1, 0:1, :] * own_first
        before = jnp.where(p > 0, before, 0.0)
        after = pick[which, 3 * (p + 1) + 2, 0:F, :]
        unit, out = ((unit_d, out_d), (unit_g, out_g))[which]
        lower, upper = (unit[0], unit[1])
        for f in range(F):
            out[f] = out[f] + before[f : f + 1, :] * lower + after[f : f + 1, :] * upper

    for k in range(1, n_yz):
        req_copy(k).wait_send()
        rep_copy(k).wait_send()
    for k in range(1, n_gx):
        gain_copy(k).wait_send()
        edge_copy(k, p, gx(k)).wait_send()

    @pl.when(p < n_gx - 1)
    def _():
        to_above().wait_send()

    @pl.when(p > 0)
    def _():
        to_below().wait_send()


def gain_from(gains, gain_s, gain_r, k, p, r, n_gx):
    rank = lax.rem(p - k + n_gx, n_gx)
    return pltpu.make_async_remote_copy(
        src_ref=gains.at[rank],
        dst_ref=gains.at[rank],
        send_sem=gain_s.at[k],
        recv_sem=gain_r.at[k],
        device_id=(rank, r),
        device_id_type=MESH,
    )


def shards(fields, target, owner, sx, col, weights, sensor):
    F, X, C = fields.shape
    G = target.shape[1]
    n_gx, n_yz = (lax.axis_size("gx"), lax.axis_size("yz"))
    GP = max(G, 128)
    pack = GP // G
    edge_rows = -(-4 * F // ROWS) * ROWS
    f32, bf16 = (jnp.float32, jnp.bfloat16)
    vmem = pl.BlockSpec(memory_space=pltpu.VMEM)
    dma = pltpu.SemaphoreType.DMA
    hbm = pl.BlockSpec(memory_space=pltpu.HBM)
    inputs = (fields, target, target, sx, col, weights, sensor)
    out = pltpu.VMEM(fields.shape, f32)
    return pl.pallas_call(
        functools.partial(kernel, n_gx, n_yz),
        out_shape=(out, out),
        in_specs=[hbm] * 7,
        out_specs=(vmem, vmem),
        scratch_shapes=[
            *[pltpu.VMEM(a.shape, a.dtype) for a in inputs],
            dma((7,)),
            pltpu.VMEM((3 * F * X, C), bf16),
            pltpu.VMEM((3 * GP, C), bf16),
            pltpu.VMEM((n_yz, ROWS, GP), f32),
            pltpu.VMEM((n_yz, ROWS, GP), f32),
            pltpu.VMEM((n_yz // pack, ROWS, GP), f32),
            pltpu.VMEM((X + 2 * HALO, ROWS, C), f32),
            pltpu.VMEM((7, X, ROWS, C), f32),
            pltpu.VMEM((n_gx, ROWS, C), f32),
            pltpu.VMEM((n_gx, edge_rows, C), f32),
            pltpu.VMEM((2, X, C), f32),
            pltpu.VMEM((2, X, C), f32),
            pltpu.VMEM((2, X, ROWS, C), f32),
            pltpu.VMEM((2, 3 * (n_gx + 1), ROWS, C), f32),
            dma((n_yz,)),
            dma((n_yz,)),
            dma((n_yz,)),
            dma((n_yz,)),
            dma((n_gx,)),
            dma((n_gx,)),
            dma((2,)),
            dma((2,)),
            dma((n_gx,)),
            dma((n_gx,)),
        ],
        compiler_params=pltpu.CompilerParams(collective_id=0, has_side_effects=True),
    )(fields, target, owner.reshape(target.shape), sx, col, weights, sensor)


def solution(mesh):
    placed = (
        P(None, "gx", "yz"),
        P("gx", "yz"),
        P("gx", "yz", None),
        P("gx", "yz"),
        P("gx", "yz"),
        P(None, "gx", "yz"),
        P("gx", "yz"),
    )
    return jax.shard_map(
        shards,
        mesh=mesh,
        in_specs=placed,
        out_specs=(P(None, "gx", "yz"), P(None, "gx", "yz")),
        check_vma=False,
    )
```

```python
import functools

import jax
import jax.numpy as jnp
from jax import lax
from jax.experimental import pallas as pl
from jax.experimental.pallas import tpu as pltpu
from jax.sharding import PartitionSpec as P

MESH = pl.DeviceIdType.MESH
SIGNS = (1.0, -1.0, 1.0, 1.0, 1.0)
ALPHA_TOP = 0.499
ALPHA_STEP = 0.006
HALO = 5
ROWS = 8


def thirds_factors(cells):
    a = 1.0 / 3.0
    link, inverse, last = ([], [], 0.0)
    for x in range(cells):
        inv = 1.0 / (1.0 - (a * last if x else 0.0))
        last = a * inv
        inverse.append(inv)
        link.append(last)
    left, right = ([0.0] * cells, [0.0] * cells)
    y = -link[0]
    left[0] = y
    for x in range(1, cells):
        y = -link[x] * y
        left[x] = y
    right[-1] = -link[-1]
    for x in range(cells - 2, -1, -1):
        left[x] = left[x] - link[x] * left[x + 1]
        right[x] = -link[x] * right[x + 1]
    return (link, inverse, left, right)


def thirds_interface(ranks, left, right):
    l0, l1, r0, r1 = (left[0], left[-1], right[0], right[-1])
    gain, out = (0.0, [])
    for q in range(ranks):
        s = 1.0 / (1.0 - l0 * gain)
        gf = r0 * s
        ng = r1 + l1 * gain * gf
        out.append((s, l0 * s, gf, l1, l1 * gain, ng))
        gain = ng
    return out


def split3(v):
    hi = v.astype(jnp.bfloat16)
    rest = v - hi.astype(jnp.float32)
    mid = rest.astype(jnp.bfloat16)
    low = (rest - mid.astype(jnp.float32)).astype(jnp.bfloat16)
    return (hi, mid, low)


def kernel(
    n_gx,
    n_yz,
    fields_hbm,
    target_hbm,
    owner_hbm,
    sx_hbm,
    col_hbm,
    weights_hbm,
    sensor_hbm,
    out_d,
    out_g,
    fields,
    target,
    owner,
    sx,
    col,
    weights,
    sensor,
    load_sem,
    parts,
    onehot_t,
    goals,
    reqs,
    reps,
    answers,
    fb,
    coef,
    gains,
    edges,
    unit_d,
    unit_g,
    sol,
    pick,
    req_s,
    req_r,
    rep_s,
    rep_r,
    goal_s,
    goal_r,
    gain_s,
    gain_r,
    halo_s,
    halo_r,
    edge_s,
    edge_r,
):
    F, X, C = fields.shape
    G = target.shape[1]
    GP = reqs.shape[2]
    pack = GP // G
    p = lax.axis_index("gx")
    r = lax.axis_index("yz")
    f32, bf16 = (jnp.float32, jnp.bfloat16)

    def yz(k):
        return (p, lax.rem(r + k + n_yz, n_yz))

    def gx(k):
        return (lax.rem(p + k + n_gx, n_gx), r)

    barrier = pltpu.get_barrier_semaphore()
    loads = [
        pltpu.make_async_copy(src, dst, load_sem.at[i])
        for i, (src, dst) in enumerate(
            (
                (owner_hbm, owner),
                (sx_hbm, sx),
                (col_hbm, col),
                (weights_hbm, weights),
                (target_hbm, target),
                (fields_hbm, fields),
                (sensor_hbm, sensor),
            )
        )
    ]
    for copy in loads:
        copy.start()
    fb[...] = jnp.zeros_like(fb)
    edges[...] = jnp.zeros_like(edges)
    reps[...] = jnp.zeros_like(reps)
    goals[...] = jnp.full(goals.shape, -1.0, f32)
    for k in range(1, n_yz):
        pl.semaphore_signal(barrier, inc=1, device_id=yz(k), device_id_type=MESH)
    for k in range(1, n_gx):
        pl.semaphore_signal(barrier, inc=1, device_id=gx(k), device_id_type=MESH)

    for copy in loads[:4]:
        copy.wait()
    reqs[0] = jnp.zeros((ROWS, GP), f32)
    reqs[0, 0:1, 0:G] = col[...].astype(f32)
    reqs[0, 1:2, 0:G] = sx[...].astype(f32)
    reqs[0, 2:3, 0:G] = owner[...].astype(f32)
    for k in range(4):
        reqs[0, 3 + k : 4 + k, 0:G] = weights[k]

    pl.semaphore_wait(barrier, n_yz - 1 + n_gx - 1)

    def req_copy(k):
        return pltpu.make_async_remote_copy(
            src_ref=reqs.at[0],
            dst_ref=reqs.at[k],
            send_sem=req_s.at[k],
            recv_sem=req_r.at[k],
            device_id=yz(k),
            device_id_type=MESH,
        )

    for k in range(1, n_yz):
        req_copy(k).start()

    def goal_copy(kind):
        return pltpu.make_async_remote_copy(
            src_ref=goals.at[0],
            dst_ref=goals.at[kind],
            send_sem=goal_s.at[kind],
            recv_sem=goal_r.at[kind],
            device_id=gx(1 if kind == 1 else -1),
            device_id_type=MESH,
        )

    def halo_copy(kind):
        return pltpu.make_async_remote_copy(
            src_ref=fb.at[pl.ds(X if kind == 1 else HALO, HALO)],
            dst_ref=fb.at[pl.ds(0 if kind == 1 else HALO + X, HALO)],
            send_sem=halo_s.at[kind],
            recv_sem=halo_r.at[kind],
            device_id=gx(1 if kind == 1 else -1),
            device_id_type=MESH,
        )

    has_above = p < n_gx - 1
    has_below = p > 0

    def each_sent(act):
        @pl.when(has_above)
        def _():
            act(1)

        @pl.when(has_below)
        def _():
            act(2)

    def each_received(act):
        @pl.when(has_below)
        def _():
            act(1)

        @pl.when(has_above)
        def _():
            act(2)

    bits = C.bit_length() - 1
    loads[4].wait()
    goal = target[...]
    goals[0, 0:1, 0:G] = jnp.right_shift(goal, bits).astype(f32)
    goals[0, 1:2, 0:G] = jnp.bitwise_and(goal, C - 1).astype(f32)
    each_sent(lambda kind: goal_copy(kind).start())

    across = lax.broadcasted_iota(jnp.int32, (GP, C), 1).astype(f32)

    def hits(kind):
        column = jnp.transpose(goals[kind])[:, 1:2]
        hit = jnp.where(across == column, 1.0, 0.0).astype(bf16)
        for i in range(3):
            onehot_t[kind, i * GP : (i + 1) * GP, :] = hit
        return hit

    loads[5].wait()
    for x in range(X):
        for f in range(F):
            fb[HALO + x, f : f + 1, :] = fields[f, x : x + 1, :]
    goal_x = jnp.broadcast_to(goals[0, 0:1, :], (ROWS, GP))
    ones = jnp.concatenate([jnp.where(goal_x == x, 1.0, 0.0) for x in range(X)], axis=0)
    taken = jnp.dot(ones.astype(bf16), hits(0), preferred_element_type=f32)
    for x in range(X):
        here = taken[x * ROWS : (x + 1) * ROWS]
        fb[HALO + x] = jnp.where(here > 0.5, 0.0, fb[HALO + x])
    each_sent(lambda kind: halo_copy(kind).start())

    flat = fields[...].reshape(F * X, C)
    for i, piece in enumerate(split3(flat)):
        parts[i * F * X : (i + 1) * F * X, :] = piece

    lane_c = lax.broadcasted_iota(jnp.int32, (C, GP), 0)
    row_x = lax.broadcasted_iota(jnp.int32, (X, GP), 0)
    own = r.astype(f32)

    def rep_copy(kind, k):
        rank = lax.rem(p + (0, 1, n_gx - 1)[kind], n_gx)
        return pltpu.make_async_remote_copy(
            src_ref=answers.at[k // pack],
            dst_ref=reps.at[kind, k],
            send_sem=rep_s.at[kind, k],
            recv_sem=rep_r.at[kind, k],
            device_id=(rank, lax.rem(r - k + n_yz, n_yz)),
            device_id_type=MESH,
        )

    for j in range(n_yz // pack):
        block = None
        for i in range(pack):
            k = j * pack + i
            if k:
                req_copy(k).wait_recv()
            piece = reqs[k]
            if i:
                piece = pltpu.roll(piece, i * G, 1)
            block = piece if block is None else block + piece
        hot = jnp.where(lane_c == block[0:1, :].astype(jnp.int32), 1.0, 0.0).astype(bf16)
        got = jnp.dot(parts[...], hot, preferred_element_type=f32)
        offset = row_x - block[1:2, :].astype(jnp.int32)
        mask = jnp.zeros((X, GP), f32)
        for k in range(4):
            mask = jnp.where(offset == k, block[3 + k : 4 + k, :], mask)
        mask = jnp.where(block[2:3, :] == own, mask, 0.0)
        n = F * X
        total = got[0:n] + got[n : 2 * n] + got[2 * n : 3 * n]
        rows = []
        for f in range(F):
            value = jnp.sum(total[f * X : (f + 1) * X] * mask, axis=0, keepdims=True)
            rows.append(SIGNS[f] * value)
        rows.append(jnp.zeros((ROWS - F, GP), f32))
        answers[j] = jnp.concatenate(rows, axis=0)
        for i in range(pack):
            k = j * pack + i
            if k:
                rep_copy(0, k).start()

        def neighbours(kind):
            for i in range(pack):
                rep_copy(kind, j * pack + i).start()

        each_sent(neighbours)

    loads[6].wait()
    link = []
    inverse = []
    for x in range(X):
        b = jnp.broadcast_to(sensor[x : x + 1, :].astype(f32), (ROWS, C))
        alpha = ALPHA_TOP - ALPHA_STEP * b
        den = jnp.ones((ROWS, C), f32) if x == 0 else 1.0 - alpha * link[-1]
        inv = 1.0 / den
        link.append(alpha * inv)
        inverse.append(inv)
        twice = 2.0 * alpha - 1.0
        coef[0, x] = inv * ((193.0 + 126.0 * alpha) / 256.0)
        coef[1, x] = inv * ((105.0 + 302.0 * alpha) / 512.0)
        scaled = inv * twice
        coef[2, x] = scaled * (15.0 / 128.0)
        coef[3, x] = scaled * (-45.0 / 1024.0)
        coef[4, x] = scaled * (5.0 / 512.0)
        coef[5, x] = scaled * (-1.0 / 1024.0)
        coef[6, x] = link[-1]
    y = [-link[0]]
    for x in range(1, X):
        y.append(-link[x] * y[-1])
    ul, ur = (y[-1], -link[-1])
    unit_g[0, X - 1 : X, :] = ul[0:1, :]
    unit_g[1, X - 1 : X, :] = ur[0:1, :]
    ends = [None, ul, None, ur]
    for x in range(X - 2, -1, -1):
        ul = y[x] - link[x] * ul
        ur = -link[x] * ur
        unit_g[0, x : x + 1, :] = ul[0:1, :]
        unit_g[1, x : x + 1, :] = ur[0:1, :]
    ends[0], ends[2] = (ul, ur)
    mine = gains.at[p]
    for i in range(4):
        mine[2 * i : 2 * i + 2, :] = ends[i][0:2, :]

    def gain_copy(k):
        return pltpu.make_async_remote_copy(
            src_ref=gains.at[p],
            dst_ref=gains.at[p],
            send_sem=gain_s.at[k],
            recv_sem=gain_r.at[k],
            device_id=gx(k),
            device_id_type=MESH,
        )

    for k in range(1, n_gx):
        gain_copy(k).start()

    link_d, inverse_d, left_d, right_d = thirds_factors(X)
    inter_d = thirds_interface(n_gx, left_d, right_d)
    for x in range(X):
        unit_d[0, x : x + 1, :] = jnp.full((1, C), left_d[x], f32)
        unit_d[1, x : x + 1, :] = jnp.full((1, C), right_d[x], f32)

    each_received(lambda kind: goal_copy(kind).wait_recv())
    hits(1)
    hits(2)

    each_sent(lambda kind: halo_copy(kind).wait_send())
    each_received(lambda kind: halo_copy(kind).wait_recv())
    for k in range(1, n_yz):
        rep_copy(0, k).wait_recv()

    def arrived(kind):
        for k in range(n_yz):
            rep_copy(kind, k).wait_recv()

    each_received(arrived)
    for kind, (start, cells) in enumerate(((0, X), (X - HALO, HALO), (0, HALO))):
        sums = [None] * pack
        for k in range(n_yz):
            piece = answers[0] if kind == 0 and k == 0 else reps[kind, k]
            i = k % pack
            sums[i] = piece if sums[i] is None else sums[i] + piece
        total = sums[0]
        for i in range(1, pack):
            total = total + pltpu.roll(sums[i], GP - i * G, 1)
        goal_x = jnp.broadcast_to(goals[kind, 0:1, :], (ROWS, GP))
        stack = []
        for piece in split3(total):
            wide = piece.astype(f32)
            stack.append(
                jnp.concatenate(
                    [jnp.where(goal_x == x, wide, 0.0) for x in range(start, start + cells)],
                    axis=0,
                )
            )
        spread = jnp.dot(
            jnp.concatenate(stack, axis=1).astype(bf16),
            onehot_t[kind],
            preferred_element_type=f32,
        )
        base = (HALO, 0, HALO + X)[kind]
        for x in range(cells):
            fb[base + x] = fb[base + x] + spread[x * ROWS : (x + 1) * ROWS]

    yd, yg = ([], [])
    for x in range(X):
        at = HALO + x
        near, next2 = (fb[at + 1], fb[at + 2])
        back, back2 = (fb[at - 1], fb[at - 2])
        slope = (7.0 / 9.0 * inverse_d[x]) * (near - back) + (1.0 / 36.0 * inverse_d[x]) * (
            next2 - back2
        )
        smooth = coef[0, x] * fb[at] + coef[1, x] * (near + back) + coef[2, x] * (next2 + back2)
        for n in range(3, 6):
            smooth = smooth + coef[n, x] * (fb[at + n] + fb[at - n])
        if x:
            slope = slope - link_d[x] * yd[-1]
            smooth = smooth - coef[6, x] * yg[-1]
        yd.append(slope)
        yg.append(smooth)
    ud, ug = (yd[-1], yg[-1])
    last_d, last_g = (ud, ug)
    sol[0, X - 1] = ud
    sol[1, X - 1] = ug
    for x in range(X - 2, -1, -1):
        ud = yd[x] - link_d[x] * ud
        ug = yg[x] - coef[6, x] * ug
        sol[0, x] = ud
        sol[1, x] = ug
    here = edges.at[p]
    for i, v in enumerate((ud, last_d, ug, last_g)):
        here[i * F : (i + 1) * F, :] = v[0:F]

    def edge_copy(k, rank, peer):
        return pltpu.make_async_remote_copy(
            src_ref=edges.at[rank],
            dst_ref=edges.at[rank],
            send_sem=edge_s.at[k],
            recv_sem=edge_r.at[k],
            device_id=peer,
            device_id_type=MESH,
        )

    for k in range(1, n_gx):
        edge_copy(k, p, gx(k)).start()

    for x in range(X):
        for f in range(F):
            out_d[f, x : x + 1, :] = sol[0, x, f : f + 1, :]
            out_g[f, x : x + 1, :] = sol[1, x, f : f + 1, :]

    inter_g = []
    gain = jnp.zeros((1, C), f32)
    for k in range(1, n_gx):
        gain_from(gains, gain_s, gain_r, k, p, r, n_gx).wait_recv()
    for q in range(n_gx):
        l0, l1 = (gains[q, 0:1, :], gains[q, 2:3, :])
        r0, r1 = (gains[q, 4:5, :], gains[q, 6:7, :])
        s = 1.0 / (1.0 - l0 * gain)
        gf = r0 * s
        ng = r1 + l1 * gain * gf
        inter_g.append((s, l0 * s, gf, l1, l1 * gain, ng))
        gain = ng

    for k in range(1, n_gx):
        edge_copy(k, lax.rem(p - k + n_gx, n_gx), gx(-k)).wait_recv()

    for which, inter in enumerate((inter_d, inter_g)):
        hold = jnp.zeros((F, C), f32)
        first = []
        pick[which, 0, 0:F, :] = hold
        pick[which, 1, 0:1, :] = jnp.zeros((1, C), f32)
        for q in range(n_gx):
            s, ls, gf, l1, lg, ng = inter[q]
            h0 = edges[q, which * 2 * F : which * 2 * F + F, :]
            h1 = edges[q, which * 2 * F + F : which * 2 * F + 2 * F, :]
            hf = s * h0 + ls * hold
            hold = h1 + l1 * hold + lg * hf
            first.append(hf)
            pick[which, 3 * (q + 1), 0:F, :] = hold
            pick[which, 3 * (q + 1) + 1, 0:1, :] = jnp.broadcast_to(jnp.asarray(ng, f32), (1, C))
        after = jnp.zeros((F, C), f32)
        pick[which, 3 * n_gx + 2, 0:F, :] = after
        for q in range(n_gx - 1, -1, -1):
            after = first[q] + inter[q][2] * after
            pick[which, 3 * q + 2, 0:F, :] = after
        own_first = pick[which, 3 * p + 2, 0:F, :]
        before = pick[which, 3 * p, 0:F, :] + pick[which, 3 * p + 1, 0:1, :] * own_first
        before = jnp.where(p > 0, before, 0.0)
        after = pick[which, 3 * (p + 1) + 2, 0:F, :]
        unit, out = ((unit_d, out_d), (unit_g, out_g))[which]
        lower, upper = (unit[0], unit[1])
        for f in range(F):
            out[f] = out[f] + before[f : f + 1, :] * lower + after[f : f + 1, :] * upper

    for k in range(1, n_yz):
        req_copy(k).wait_send()
        rep_copy(0, k).wait_send()
    for k in range(1, n_gx):
        gain_copy(k).wait_send()
        edge_copy(k, p, gx(k)).wait_send()

    def sent(kind):
        goal_copy(kind).wait_send()
        for k in range(n_yz):
            rep_copy(kind, k).wait_send()

    each_sent(sent)


def gain_from(gains, gain_s, gain_r, k, p, r, n_gx):
    rank = lax.rem(p - k + n_gx, n_gx)
    return pltpu.make_async_remote_copy(
        src_ref=gains.at[rank],
        dst_ref=gains.at[rank],
        send_sem=gain_s.at[k],
        recv_sem=gain_r.at[k],
        device_id=(rank, r),
        device_id_type=MESH,
    )


def shards(fields, target, owner, sx, col, weights, sensor):
    F, X, C = fields.shape
    G = target.shape[1]
    n_gx, n_yz = (lax.axis_size("gx"), lax.axis_size("yz"))
    GP = max(G, 128)
    pack = GP // G
    edge_rows = -(-4 * F // ROWS) * ROWS
    f32, bf16 = (jnp.float32, jnp.bfloat16)
    vmem = pl.BlockSpec(memory_space=pltpu.VMEM)
    dma = pltpu.SemaphoreType.DMA
    hbm = pl.BlockSpec(memory_space=pltpu.HBM)
    inputs = (fields, target, target, sx, col, weights, sensor)
    out = pltpu.VMEM(fields.shape, f32)
    return pl.pallas_call(
        functools.partial(kernel, n_gx, n_yz),
        out_shape=(out, out),
        in_specs=[hbm] * 7,
        out_specs=(vmem, vmem),
        scratch_shapes=[
            *[pltpu.VMEM(a.shape, a.dtype) for a in inputs],
            dma((7,)),
            pltpu.VMEM((3 * F * X, C), bf16),
            pltpu.VMEM((3, 3 * GP, C), bf16),
            pltpu.VMEM((3, ROWS, GP), f32),
            pltpu.VMEM((n_yz, ROWS, GP), f32),
            pltpu.VMEM((3, n_yz, ROWS, GP), f32),
            pltpu.VMEM((n_yz // pack, ROWS, GP), f32),
            pltpu.VMEM((X + 2 * HALO, ROWS, C), f32),
            pltpu.VMEM((7, X, ROWS, C), f32),
            pltpu.VMEM((n_gx, ROWS, C), f32),
            pltpu.VMEM((n_gx, edge_rows, C), f32),
            pltpu.VMEM((2, X, C), f32),
            pltpu.VMEM((2, X, C), f32),
            pltpu.VMEM((2, X, ROWS, C), f32),
            pltpu.VMEM((2, 3 * (n_gx + 1), ROWS, C), f32),
            dma((n_yz,)),
            dma((n_yz,)),
            dma((3, n_yz)),
            dma((3, n_yz)),
            dma((3,)),
            dma((3,)),
            dma((n_gx,)),
            dma((n_gx,)),
            dma((3,)),
            dma((3,)),
            dma((n_gx,)),
            dma((n_gx,)),
        ],
        compiler_params=pltpu.CompilerParams(collective_id=0, has_side_effects=True),
    )(fields, target, owner.reshape(target.shape), sx, col, weights, sensor)


def solution(mesh):
    placed = (
        P(None, "gx", "yz"),
        P("gx", "yz"),
        P("gx", "yz", None),
        P("gx", "yz"),
        P("gx", "yz"),
        P(None, "gx", "yz"),
        P("gx", "yz"),
    )
    return jax.shard_map(
        shards,
        mesh=mesh,
        in_specs=placed,
        out_specs=(P(None, "gx", "yz"), P(None, "gx", "yz")),
        check_vma=False,
    )
```

```python
import functools

import jax
import jax.numpy as jnp
from jax import lax
from jax.experimental import pallas as pl
from jax.experimental.pallas import tpu as pltpu
from jax.sharding import PartitionSpec as P

MESH = pl.DeviceIdType.MESH
SIGNS = (1.0, -1.0, 1.0, 1.0, 1.0)
ALPHA_TOP = 0.499
ALPHA_STEP = 0.006
HALO = 5
ROWS = 8


def thirds_factors(cells):
    a = 1.0 / 3.0
    link, inverse, last = ([], [], 0.0)
    for x in range(cells):
        inv = 1.0 / (1.0 - (a * last if x else 0.0))
        last = a * inv
        inverse.append(inv)
        link.append(last)
    left, right = ([0.0] * cells, [0.0] * cells)
    y = -link[0]
    left[0] = y
    for x in range(1, cells):
        y = -link[x] * y
        left[x] = y
    right[-1] = -link[-1]
    for x in range(cells - 2, -1, -1):
        left[x] = left[x] - link[x] * left[x + 1]
        right[x] = -link[x] * right[x + 1]
    return (link, inverse, left, right)


def thirds_interface(ranks, left, right):
    l0, l1, r0, r1 = (left[0], left[-1], right[0], right[-1])
    gain, out = (0.0, [])
    for q in range(ranks):
        s = 1.0 / (1.0 - l0 * gain)
        gf = r0 * s
        ng = r1 + l1 * gain * gf
        out.append((s, l0 * s, gf, l1, l1 * gain, ng))
        gain = ng
    return out


def split3(v):
    hi = v.astype(jnp.bfloat16)
    rest = v - hi.astype(jnp.float32)
    mid = rest.astype(jnp.bfloat16)
    low = (rest - mid.astype(jnp.float32)).astype(jnp.bfloat16)
    return (hi, mid, low)


def kernel(
    n_gx,
    n_yz,
    fields_hbm,
    target_hbm,
    owner_hbm,
    sx_hbm,
    col_hbm,
    weights_hbm,
    sensor_hbm,
    out_d,
    out_g,
    units,
    ends,
    fields,
    target,
    owner,
    sx,
    col,
    weights,
    sensor,
    load_sem,
    parts,
    onehot_t,
    goals,
    reqs,
    reps,
    answers,
    fb,
    coef,
    gains,
    edges,
    sol,
    pick,
    req_s,
    req_r,
    rep_s,
    rep_r,
    goal_s,
    goal_r,
    gain_s,
    gain_r,
    halo_s,
    halo_r,
    edge_s,
    edge_r,
):
    F, X, C = fields.shape
    G = target.shape[1]
    GP = reqs.shape[2]
    pack = GP // G
    p = lax.axis_index("gx")
    r = lax.axis_index("yz")
    f32, bf16 = (jnp.float32, jnp.bfloat16)

    def yz(k):
        return (p, lax.rem(r + k + n_yz, n_yz))

    def gx(k):
        return (lax.rem(p + k + n_gx, n_gx), r)

    barrier = pltpu.get_barrier_semaphore()
    for k in range(1, n_yz):
        pl.semaphore_signal(barrier, inc=1, device_id=yz(k), device_id_type=MESH)
    for k in range(1, n_gx):
        pl.semaphore_signal(barrier, inc=1, device_id=gx(k), device_id_type=MESH)
    loads = [
        pltpu.make_async_copy(src, dst, load_sem.at[i])
        for i, (src, dst) in enumerate(
            (
                (owner_hbm, owner),
                (sx_hbm, sx),
                (col_hbm, col),
                (weights_hbm, weights),
                (target_hbm, target),
                (fields_hbm, fields),
                (sensor_hbm, sensor),
            )
        )
    ]
    for copy in loads:
        copy.start()
    goals[0] = jnp.full((ROWS, GP), -1.0, f32)
    for x in range(X):
        fb[HALO + x] = jnp.zeros((ROWS, C), f32)

    def absent(kind, base):
        goals[kind] = jnp.full((ROWS, GP), -1.0, f32)
        fb[base : base + HALO] = jnp.zeros((HALO, ROWS, C), f32)
        reps[kind] = jnp.zeros((n_yz, ROWS, GP), f32)

    @pl.when(p == 0)
    def _():
        absent(1, 0)

    @pl.when(p == n_gx - 1)
    def _():
        absent(2, HALO + X)

    for copy in loads[:4]:
        copy.wait()
    reqs[0] = jnp.zeros((ROWS, GP), f32)
    reqs[0, 0:1, 0:G] = col[...].astype(f32)
    reqs[0, 1:2, 0:G] = sx[...].astype(f32)
    reqs[0, 2:3, 0:G] = owner[...].astype(f32)
    for k in range(4):
        reqs[0, 3 + k : 4 + k, 0:G] = weights[k]

    pl.semaphore_wait(barrier, n_yz - 1 + n_gx - 1)

    def req_copy(k):
        return pltpu.make_async_remote_copy(
            src_ref=reqs.at[0],
            dst_ref=reqs.at[k],
            send_sem=req_s.at[k],
            recv_sem=req_r.at[k],
            device_id=yz(k),
            device_id_type=MESH,
        )

    for k in range(1, n_yz):
        req_copy(k).start()

    def goal_copy(kind):
        return pltpu.make_async_remote_copy(
            src_ref=goals.at[0],
            dst_ref=goals.at[kind],
            send_sem=goal_s.at[kind],
            recv_sem=goal_r.at[kind],
            device_id=gx(1 if kind == 1 else -1),
            device_id_type=MESH,
        )

    def halo_copy(kind):
        return pltpu.make_async_remote_copy(
            src_ref=fb.at[pl.ds(X if kind == 1 else HALO, HALO)],
            dst_ref=fb.at[pl.ds(0 if kind == 1 else HALO + X, HALO)],
            send_sem=halo_s.at[kind],
            recv_sem=halo_r.at[kind],
            device_id=gx(1 if kind == 1 else -1),
            device_id_type=MESH,
        )

    has_above = p < n_gx - 1
    has_below = p > 0

    def each_sent(act):
        @pl.when(has_above)
        def _():
            act(1)

        @pl.when(has_below)
        def _():
            act(2)

    def each_received(act):
        @pl.when(has_below)
        def _():
            act(1)

        @pl.when(has_above)
        def _():
            act(2)

    bits = C.bit_length() - 1
    loads[4].wait()
    goal = target[...]
    goals[0, 0:1, 0:G] = jnp.right_shift(goal, bits).astype(f32)
    goals[0, 1:2, 0:G] = jnp.bitwise_and(goal, C - 1).astype(f32)
    each_sent(lambda kind: goal_copy(kind).start())

    across = lax.broadcasted_iota(jnp.int32, (GP, C), 1).astype(f32)

    def hits(kind):
        column = jnp.transpose(goals[kind])[:, 1:2]
        hit = jnp.where(across == column, 1.0, 0.0).astype(bf16)
        for i in range(3):
            onehot_t[kind, i * GP : (i + 1) * GP, :] = hit
        return hit

    loads[5].wait()
    for x in range(X):
        for f in range(F):
            fb[HALO + x, f : f + 1, :] = fields[f, x : x + 1, :]
    goal_x = jnp.broadcast_to(goals[0, 0:1, :], (ROWS, GP))
    ones = jnp.concatenate([jnp.where(goal_x == x, 1.0, 0.0) for x in range(X)], axis=0)
    taken = jnp.dot(ones.astype(bf16), hits(0), preferred_element_type=f32)
    for x in range(X):
        here = taken[x * ROWS : (x + 1) * ROWS]
        fb[HALO + x] = jnp.where(here > 0.5, 0.0, fb[HALO + x])
    each_sent(lambda kind: halo_copy(kind).start())

    flat = fields[...].reshape(F * X, C)
    for i, piece in enumerate(split3(flat)):
        parts[i * F * X : (i + 1) * F * X, :] = piece

    lane_c = lax.broadcasted_iota(jnp.int32, (C, GP), 0)
    row_x = lax.broadcasted_iota(jnp.int32, (X, GP), 0)
    own = r.astype(f32)

    def rep_copy(kind, k):
        rank = lax.rem(p + (0, 1, n_gx - 1)[kind], n_gx)
        return pltpu.make_async_remote_copy(
            src_ref=answers.at[k // pack],
            dst_ref=reps.at[kind, k],
            send_sem=rep_s.at[kind, k],
            recv_sem=rep_r.at[kind, k],
            device_id=(rank, lax.rem(r - k + n_yz, n_yz)),
            device_id_type=MESH,
        )

    for j in range(n_yz // pack):
        block = None
        for i in range(pack):
            k = j * pack + i
            if k:
                req_copy(k).wait_recv()
            piece = reqs[k]
            if i:
                piece = pltpu.roll(piece, i * G, 1)
            block = piece if block is None else block + piece
        hot = jnp.where(lane_c == block[0:1, :].astype(jnp.int32), 1.0, 0.0).astype(bf16)
        got = jnp.dot(parts[...], hot, preferred_element_type=f32)
        offset = row_x - block[1:2, :].astype(jnp.int32)
        mask = jnp.zeros((X, GP), f32)
        for k in range(4):
            mask = jnp.where(offset == k, block[3 + k : 4 + k, :], mask)
        mask = jnp.where(block[2:3, :] == own, mask, 0.0)
        n = F * X
        total = got[0:n] + got[n : 2 * n] + got[2 * n : 3 * n]
        rows = []
        for f in range(F):
            value = jnp.sum(total[f * X : (f + 1) * X] * mask, axis=0, keepdims=True)
            rows.append(SIGNS[f] * value)
        rows.append(jnp.zeros((ROWS - F, GP), f32))
        answers[j] = jnp.concatenate(rows, axis=0)
        for i in range(pack):
            k = j * pack + i
            if k:
                rep_copy(0, k).start()

        def neighbours(kind):
            for i in range(pack):
                rep_copy(kind, j * pack + i).start()

        each_sent(neighbours)

    loads[6].wait()
    link = []
    inverse = []
    for x in range(X):
        b = jnp.broadcast_to(sensor[x : x + 1, :].astype(f32), (ROWS, C))
        alpha = ALPHA_TOP - ALPHA_STEP * b
        den = jnp.ones((ROWS, C), f32) if x == 0 else 1.0 - alpha * link[-1]
        inv = 1.0 / den
        link.append(alpha * inv)
        inverse.append(inv)
        twice = 2.0 * alpha - 1.0
        coef[0, x] = inv * ((193.0 + 126.0 * alpha) / 256.0)
        coef[1, x] = inv * ((105.0 + 302.0 * alpha) / 512.0)
        scaled = inv * twice
        coef[2, x] = scaled * (15.0 / 128.0)
        coef[3, x] = scaled * (-45.0 / 1024.0)
        coef[4, x] = scaled * (5.0 / 512.0)
        coef[5, x] = scaled * (-1.0 / 1024.0)
        coef[6, x] = link[-1]
    y = [-link[0]]
    for x in range(1, X):
        y.append(-link[x] * y[-1])
    ul, ur = (y[-1], -link[-1])
    units[2, X - 1 : X, :] = ul[0:1, :]
    units[3, X - 1 : X, :] = ur[0:1, :]
    tips = [None, ul, None, ur]
    for x in range(X - 2, -1, -1):
        ul = y[x] - link[x] * ul
        ur = -link[x] * ur
        units[2, x : x + 1, :] = ul[0:1, :]
        units[3, x : x + 1, :] = ur[0:1, :]
    tips[0], tips[2] = (ul, ur)
    mine = gains.at[p]
    for i in range(4):
        mine[2 * i : 2 * i + 2, :] = tips[i][0:2, :]

    def gain_copy(k):
        return pltpu.make_async_remote_copy(
            src_ref=gains.at[p],
            dst_ref=gains.at[p],
            send_sem=gain_s.at[k],
            recv_sem=gain_r.at[k],
            device_id=gx(k),
            device_id_type=MESH,
        )

    for k in range(1, n_gx):
        gain_copy(k).start()

    link_d, inverse_d, left_d, right_d = thirds_factors(X)
    inter_d = thirds_interface(n_gx, left_d, right_d)
    for x in range(X):
        units[0, x : x + 1, :] = jnp.full((1, C), left_d[x], f32)
        units[1, x : x + 1, :] = jnp.full((1, C), right_d[x], f32)

    each_received(lambda kind: goal_copy(kind).wait_recv())
    hits(1)
    hits(2)

    each_sent(lambda kind: halo_copy(kind).wait_send())
    each_received(lambda kind: halo_copy(kind).wait_recv())
    for k in range(1, n_yz):
        rep_copy(0, k).wait_recv()

    def arrived(kind):
        for k in range(n_yz):
            rep_copy(kind, k).wait_recv()

    each_received(arrived)
    for kind, (start, cells) in enumerate(((0, X), (X - HALO, HALO), (0, HALO))):
        sums = [None] * pack
        for k in range(n_yz):
            piece = answers[0] if kind == 0 and k == 0 else reps[kind, k]
            i = k % pack
            sums[i] = piece if sums[i] is None else sums[i] + piece
        total = sums[0]
        for i in range(1, pack):
            total = total + pltpu.roll(sums[i], GP - i * G, 1)
        goal_x = jnp.broadcast_to(goals[kind, 0:1, :], (ROWS, GP))
        stack = []
        for piece in split3(total):
            wide = piece.astype(f32)
            stack.append(
                jnp.concatenate(
                    [jnp.where(goal_x == x, wide, 0.0) for x in range(start, start + cells)],
                    axis=0,
                )
            )
        spread = jnp.dot(
            jnp.concatenate(stack, axis=1).astype(bf16),
            onehot_t[kind],
            preferred_element_type=f32,
        )
        base = (HALO, 0, HALO + X)[kind]
        for x in range(cells):
            fb[base + x] = fb[base + x] + spread[x * ROWS : (x + 1) * ROWS]

    yd, yg = ([], [])
    for x in range(X):
        at = HALO + x
        near, next2 = (fb[at + 1], fb[at + 2])
        back, back2 = (fb[at - 1], fb[at - 2])
        slope = (7.0 / 9.0 * inverse_d[x]) * (near - back) + (1.0 / 36.0 * inverse_d[x]) * (
            next2 - back2
        )
        smooth = coef[0, x] * fb[at] + coef[1, x] * (near + back) + coef[2, x] * (next2 + back2)
        for n in range(3, 6):
            smooth = smooth + coef[n, x] * (fb[at + n] + fb[at - n])
        if x:
            slope = slope - link_d[x] * yd[-1]
            smooth = smooth - coef[6, x] * yg[-1]
        yd.append(slope)
        yg.append(smooth)
    ud, ug = (yd[-1], yg[-1])
    last_d, last_g = (ud, ug)
    sol[0, X - 1] = ud
    sol[1, X - 1] = ug
    for x in range(X - 2, -1, -1):
        ud = yd[x] - link_d[x] * ud
        ug = yg[x] - coef[6, x] * ug
        sol[0, x] = ud
        sol[1, x] = ug
    here = edges.at[p]
    here[...] = jnp.zeros_like(here)
    for i, v in enumerate((ud, last_d, ug, last_g)):
        here[i * F : (i + 1) * F, :] = v[0:F]

    def edge_copy(k, rank, peer):
        return pltpu.make_async_remote_copy(
            src_ref=edges.at[rank],
            dst_ref=edges.at[rank],
            send_sem=edge_s.at[k],
            recv_sem=edge_r.at[k],
            device_id=peer,
            device_id_type=MESH,
        )

    for k in range(1, n_gx):
        edge_copy(k, p, gx(k)).start()

    for x in range(X):
        for f in range(F):
            out_d[f, x : x + 1, :] = sol[0, x, f : f + 1, :]
            out_g[f, x : x + 1, :] = sol[1, x, f : f + 1, :]

    inter_g = []
    gain = jnp.zeros((1, C), f32)
    for k in range(1, n_gx):
        gain_from(gains, gain_s, gain_r, k, p, r, n_gx).wait_recv()
    for q in range(n_gx):
        l0, l1 = (gains[q, 0:1, :], gains[q, 2:3, :])
        r0, r1 = (gains[q, 4:5, :], gains[q, 6:7, :])
        s = 1.0 / (1.0 - l0 * gain)
        gf = r0 * s
        ng = r1 + l1 * gain * gf
        inter_g.append((s, l0 * s, gf, l1, l1 * gain, ng))
        gain = ng

    for k in range(1, n_gx):
        edge_copy(k, lax.rem(p - k + n_gx, n_gx), gx(-k)).wait_recv()

    for which, inter in enumerate((inter_d, inter_g)):
        hold = jnp.zeros((F, C), f32)
        first = []
        pick[which, 0, 0:F, :] = hold
        pick[which, 1, 0:1, :] = jnp.zeros((1, C), f32)
        for q in range(n_gx):
            s, ls, gf, l1, lg, ng = inter[q]
            h0 = edges[q, which * 2 * F : which * 2 * F + F, :]
            h1 = edges[q, which * 2 * F + F : which * 2 * F + 2 * F, :]
            hf = s * h0 + ls * hold
            hold = h1 + l1 * hold + lg * hf
            first.append(hf)
            pick[which, 3 * (q + 1), 0:F, :] = hold
            pick[which, 3 * (q + 1) + 1, 0:1, :] = jnp.broadcast_to(jnp.asarray(ng, f32), (1, C))
        after = jnp.zeros((F, C), f32)
        pick[which, 3 * n_gx + 2, 0:F, :] = after
        for q in range(n_gx - 1, -1, -1):
            after = first[q] + inter[q][2] * after
            pick[which, 3 * q + 2, 0:F, :] = after
        own_first = pick[which, 3 * p + 2, 0:F, :]
        before = pick[which, 3 * p, 0:F, :] + pick[which, 3 * p + 1, 0:1, :] * own_first
        before = jnp.where(p > 0, before, 0.0)
        after = pick[which, 3 * (p + 1) + 2, 0:F, :]
        ends[2 * which] = before
        ends[2 * which + 1] = after

    for k in range(1, n_yz):
        req_copy(k).wait_send()
        rep_copy(0, k).wait_send()
    for k in range(1, n_gx):
        gain_copy(k).wait_send()
        edge_copy(k, p, gx(k)).wait_send()

    def sent(kind):
        goal_copy(kind).wait_send()
        for k in range(n_yz):
            rep_copy(kind, k).wait_send()

    each_sent(sent)


def gain_from(gains, gain_s, gain_r, k, p, r, n_gx):
    rank = lax.rem(p - k + n_gx, n_gx)
    return pltpu.make_async_remote_copy(
        src_ref=gains.at[rank],
        dst_ref=gains.at[rank],
        send_sem=gain_s.at[k],
        recv_sem=gain_r.at[k],
        device_id=(rank, r),
        device_id_type=MESH,
    )


def shards(fields, target, owner, sx, col, weights, sensor):
    F, X, C = fields.shape
    G = target.shape[1]
    n_gx, n_yz = (lax.axis_size("gx"), lax.axis_size("yz"))
    GP = max(G, 128)
    pack = GP // G
    edge_rows = -(-4 * F // ROWS) * ROWS
    f32, bf16 = (jnp.float32, jnp.bfloat16)
    vmem = pl.BlockSpec(memory_space=pltpu.VMEM)
    dma = pltpu.SemaphoreType.DMA
    hbm = pl.BlockSpec(memory_space=pltpu.HBM)
    inputs = (fields, target, target, sx, col, weights, sensor)
    out = pltpu.VMEM(fields.shape, f32)
    found = pl.pallas_call(
        functools.partial(kernel, n_gx, n_yz),
        out_shape=(out, out, pltpu.VMEM((4, X, C), f32), pltpu.VMEM((4, F, C), f32)),
        in_specs=[hbm] * 7,
        out_specs=(vmem, vmem, vmem, vmem),
        scratch_shapes=[
            *[pltpu.VMEM(a.shape, a.dtype) for a in inputs],
            dma((7,)),
            pltpu.VMEM((3 * F * X, C), bf16),
            pltpu.VMEM((3, 3 * GP, C), bf16),
            pltpu.VMEM((3, ROWS, GP), f32),
            pltpu.VMEM((n_yz, ROWS, GP), f32),
            pltpu.VMEM((3, n_yz, ROWS, GP), f32),
            pltpu.VMEM((n_yz // pack, ROWS, GP), f32),
            pltpu.VMEM((X + 2 * HALO, ROWS, C), f32),
            pltpu.VMEM((7, X, ROWS, C), f32),
            pltpu.VMEM((n_gx, ROWS, C), f32),
            pltpu.VMEM((n_gx, edge_rows, C), f32),
            pltpu.VMEM((2, X, ROWS, C), f32),
            pltpu.VMEM((2, 3 * (n_gx + 1), ROWS, C), f32),
            dma((n_yz,)),
            dma((n_yz,)),
            dma((3, n_yz)),
            dma((3, n_yz)),
            dma((3,)),
            dma((3,)),
            dma((n_gx,)),
            dma((n_gx,)),
            dma((3,)),
            dma((3,)),
            dma((n_gx,)),
            dma((n_gx,)),
        ],
        compiler_params=pltpu.CompilerParams(collective_id=0, has_side_effects=True),
    )(fields, target, owner.reshape(target.shape), sx, col, weights, sensor)
    own_d, own_g, units, ends = found

    def whole(local, i):
        low = ends[2 * i][:, None, :] * units[2 * i][None]
        return local + low + ends[2 * i + 1][:, None, :] * units[2 * i + 1][None]

    return (whole(own_d, 0), whole(own_g, 1))


def solution(mesh):
    placed = (
        P(None, "gx", "yz"),
        P("gx", "yz"),
        P("gx", "yz", None),
        P("gx", "yz"),
        P("gx", "yz"),
        P(None, "gx", "yz"),
        P("gx", "yz"),
    )
    return jax.shard_map(
        shards,
        mesh=mesh,
        in_specs=placed,
        out_specs=(P(None, "gx", "yz"), P(None, "gx", "yz")),
        check_vma=False,
    )
```

```python
import functools

import jax
import jax.numpy as jnp
from jax import lax
from jax.experimental import pallas as pl
from jax.experimental.pallas import tpu as pltpu
from jax.sharding import PartitionSpec as P

MESH = pl.DeviceIdType.MESH
SIGNS = (1.0, -1.0, 1.0, 1.0, 1.0)
ALPHA_TOP = 0.499
ALPHA_STEP = 0.006
HALO = 5
ROWS = 8


def thirds_factors(cells):
    a = 1.0 / 3.0
    link, inverse, last = ([], [], 0.0)
    for x in range(cells):
        inv = 1.0 / (1.0 - (a * last if x else 0.0))
        last = a * inv
        inverse.append(inv)
        link.append(last)
    left, right = ([0.0] * cells, [0.0] * cells)
    y = -link[0]
    left[0] = y
    for x in range(1, cells):
        y = -link[x] * y
        left[x] = y
    right[-1] = -link[-1]
    for x in range(cells - 2, -1, -1):
        left[x] = left[x] - link[x] * left[x + 1]
        right[x] = -link[x] * right[x + 1]
    return (link, inverse, left, right)


def thirds_interface(ranks, left, right):
    l0, l1, r0, r1 = (left[0], left[-1], right[0], right[-1])
    gain, out = (0.0, [])
    for q in range(ranks):
        s = 1.0 / (1.0 - l0 * gain)
        gf = r0 * s
        ng = r1 + l1 * gain * gf
        out.append((s, l0 * s, gf, l1, l1 * gain, ng))
        gain = ng
    return out


def split3(v):
    hi = v.astype(jnp.bfloat16)
    rest = v - hi.astype(jnp.float32)
    mid = rest.astype(jnp.bfloat16)
    low = (rest - mid.astype(jnp.float32)).astype(jnp.bfloat16)
    return (hi, mid, low)


def kernel(
    n_gx,
    n_yz,
    fields_hbm,
    target_hbm,
    owner_hbm,
    sx_hbm,
    col_hbm,
    weights_hbm,
    sensor_hbm,
    out_d,
    out_g,
    units,
    ends,
    fields,
    target,
    owner,
    sx,
    col,
    weights,
    sensor,
    load_sem,
    parts,
    onehot_t,
    goals,
    reqs,
    reps,
    answers,
    fb,
    coef,
    gains,
    edges,
    sol,
    pick,
    req_s,
    req_r,
    rep_s,
    rep_r,
    goal_s,
    goal_r,
    gain_s,
    gain_r,
    halo_s,
    halo_r,
    edge_s,
    edge_r,
):
    F, X, C = fields.shape
    G = target.shape[1]
    GP = reqs.shape[2]
    pack = GP // G
    p = lax.axis_index("gx")
    r = lax.axis_index("yz")
    f32, bf16 = (jnp.float32, jnp.bfloat16)

    def yz(k):
        return (p, lax.rem(r + k + n_yz, n_yz))

    def gx(k):
        return (lax.rem(p + k + n_gx, n_gx), r)

    barrier = pltpu.get_barrier_semaphore()
    for k in range(1, n_yz):
        pl.semaphore_signal(barrier, inc=1, device_id=yz(k), device_id_type=MESH)
    for k in range(1, n_gx):
        pl.semaphore_signal(barrier, inc=1, device_id=gx(k), device_id_type=MESH)
    loads = [
        pltpu.make_async_copy(src, dst, load_sem.at[i])
        for i, (src, dst) in enumerate(
            (
                (owner_hbm, owner),
                (sx_hbm, sx),
                (col_hbm, col),
                (weights_hbm, weights),
                (target_hbm, target),
                (fields_hbm, fields),
                (sensor_hbm, sensor),
            )
        )
    ]
    for copy in loads:
        copy.start()
    goals[0] = jnp.full((ROWS, GP), -1.0, f32)
    for x in range(X):
        fb[HALO + x] = jnp.zeros((ROWS, C), f32)

    def absent(kind, base):
        goals[kind] = jnp.full((ROWS, GP), -1.0, f32)
        fb[base : base + HALO] = jnp.zeros((HALO, ROWS, C), f32)
        reps[kind] = jnp.zeros((n_yz, ROWS, GP), f32)

    @pl.when(p == 0)
    def _():
        absent(1, 0)

    @pl.when(p == n_gx - 1)
    def _():
        absent(2, HALO + X)

    for copy in loads[:4]:
        copy.wait()
    reqs[0] = jnp.zeros((ROWS, GP), f32)
    reqs[0, 0:1, 0:G] = col[...].astype(f32)
    reqs[0, 1:2, 0:G] = sx[...].astype(f32)
    reqs[0, 2:3, 0:G] = owner[...].astype(f32)
    for k in range(4):
        reqs[0, 3 + k : 4 + k, 0:G] = weights[k]

    pl.semaphore_wait(barrier, n_yz - 1 + n_gx - 1)

    def req_copy(k):
        return pltpu.make_async_remote_copy(
            src_ref=reqs.at[0],
            dst_ref=reqs.at[k],
            send_sem=req_s.at[k],
            recv_sem=req_r.at[k],
            device_id=yz(k),
            device_id_type=MESH,
        )

    for k in range(1, n_yz):
        req_copy(k).start()

    def goal_copy(kind):
        return pltpu.make_async_remote_copy(
            src_ref=goals.at[0],
            dst_ref=goals.at[kind],
            send_sem=goal_s.at[kind],
            recv_sem=goal_r.at[kind],
            device_id=gx(1 if kind == 1 else -1),
            device_id_type=MESH,
        )

    def halo_copy(kind):
        return pltpu.make_async_remote_copy(
            src_ref=fb.at[pl.ds(X if kind == 1 else HALO, HALO)],
            dst_ref=fb.at[pl.ds(0 if kind == 1 else HALO + X, HALO)],
            send_sem=halo_s.at[kind],
            recv_sem=halo_r.at[kind],
            device_id=gx(1 if kind == 1 else -1),
            device_id_type=MESH,
        )

    has_above = p < n_gx - 1
    has_below = p > 0

    def each_sent(act):
        @pl.when(has_above)
        def _():
            act(1)

        @pl.when(has_below)
        def _():
            act(2)

    def each_received(act):
        @pl.when(has_below)
        def _():
            act(1)

        @pl.when(has_above)
        def _():
            act(2)

    bits = C.bit_length() - 1
    loads[4].wait()
    goal = target[...]
    goals[0, 0:1, 0:G] = jnp.right_shift(goal, bits).astype(f32)
    goals[0, 1:2, 0:G] = jnp.bitwise_and(goal, C - 1).astype(f32)
    each_sent(lambda kind: goal_copy(kind).start())

    across = lax.broadcasted_iota(jnp.int32, (GP, C), 1).astype(f32)

    def hits(kind):
        column = jnp.transpose(goals[kind])[:, 1:2]
        hit = jnp.where(across == column, 1.0, 0.0).astype(bf16)
        for i in range(3):
            onehot_t[kind, i * GP : (i + 1) * GP, :] = hit
        return hit

    loads[5].wait()
    for x in range(X):
        for f in range(F):
            fb[HALO + x, f : f + 1, :] = fields[f, x : x + 1, :]
    goal_x = jnp.broadcast_to(goals[0, 0:1, :], (ROWS, GP))
    ones = jnp.concatenate([jnp.where(goal_x == x, 1.0, 0.0) for x in range(X)], axis=0)
    taken = jnp.dot(ones.astype(bf16), hits(0), preferred_element_type=f32)
    for x in range(X):
        here = taken[x * ROWS : (x + 1) * ROWS]
        fb[HALO + x] = jnp.where(here > 0.5, 0.0, fb[HALO + x])
    each_sent(lambda kind: halo_copy(kind).start())

    flat = fields[...].reshape(F * X, C)
    for i, piece in enumerate(split3(flat)):
        parts[i * F * X : (i + 1) * F * X, :] = piece

    lane_c = lax.broadcasted_iota(jnp.int32, (C, GP), 0)
    row_x = lax.broadcasted_iota(jnp.int32, (X, GP), 0)
    own = r.astype(f32)

    def rep_copy(kind, k):
        rank = lax.rem(p + (0, 1, n_gx - 1)[kind], n_gx)
        return pltpu.make_async_remote_copy(
            src_ref=answers.at[k // pack],
            dst_ref=reps.at[kind, k],
            send_sem=rep_s.at[kind, k],
            recv_sem=rep_r.at[kind],
            device_id=(rank, lax.rem(r - k + n_yz, n_yz)),
            device_id_type=MESH,
        )

    for j in range(n_yz // pack):
        block = None
        for i in range(pack):
            k = j * pack + i
            if k:
                req_copy(k).wait_recv()
            piece = reqs[k]
            if i:
                piece = pltpu.roll(piece, i * G, 1)
            block = piece if block is None else block + piece
        hot = jnp.where(lane_c == block[0:1, :].astype(jnp.int32), 1.0, 0.0).astype(bf16)
        got = jnp.dot(parts[...], hot, preferred_element_type=f32)
        offset = row_x - block[1:2, :].astype(jnp.int32)
        mask = jnp.zeros((X, GP), f32)
        for k in range(4):
            mask = jnp.where(offset == k, block[3 + k : 4 + k, :], mask)
        mask = jnp.where(block[2:3, :] == own, mask, 0.0)
        n = F * X
        total = got[0:n] + got[n : 2 * n] + got[2 * n : 3 * n]
        rows = []
        for f in range(F):
            value = jnp.sum(total[f * X : (f + 1) * X] * mask, axis=0, keepdims=True)
            rows.append(SIGNS[f] * value)
        rows.append(jnp.zeros((ROWS - F, GP), f32))
        answers[j] = jnp.concatenate(rows, axis=0)
        for i in range(pack):
            k = j * pack + i
            if k:
                rep_copy(0, k).start()

        def neighbours(kind):
            for i in range(pack):
                rep_copy(kind, j * pack + i).start()

        each_sent(neighbours)

    loads[6].wait()
    link = []
    inverse = []
    for x in range(X):
        b = jnp.broadcast_to(sensor[x : x + 1, :].astype(f32), (ROWS, C))
        alpha = ALPHA_TOP - ALPHA_STEP * b
        den = jnp.ones((ROWS, C), f32) if x == 0 else 1.0 - alpha * link[-1]
        inv = 1.0 / den
        link.append(alpha * inv)
        inverse.append(inv)
        twice = 2.0 * alpha - 1.0
        coef[0, x] = inv * ((193.0 + 126.0 * alpha) / 256.0)
        coef[1, x] = inv * ((105.0 + 302.0 * alpha) / 512.0)
        scaled = inv * twice
        coef[2, x] = scaled * (15.0 / 128.0)
        coef[3, x] = scaled * (-45.0 / 1024.0)
        coef[4, x] = scaled * (5.0 / 512.0)
        coef[5, x] = scaled * (-1.0 / 1024.0)
        coef[6, x] = link[-1]
    y = [-link[0]]
    for x in range(1, X):
        y.append(-link[x] * y[-1])
    ul, ur = (y[-1], -link[-1])
    units[2, X - 1 : X, :] = ul[0:1, :]
    units[3, X - 1 : X, :] = ur[0:1, :]
    tips = [None, ul, None, ur]
    for x in range(X - 2, -1, -1):
        ul = y[x] - link[x] * ul
        ur = -link[x] * ur
        units[2, x : x + 1, :] = ul[0:1, :]
        units[3, x : x + 1, :] = ur[0:1, :]
    tips[0], tips[2] = (ul, ur)
    mine = gains.at[p]
    for i in range(4):
        mine[2 * i : 2 * i + 2, :] = tips[i][0:2, :]

    def gain_copy(k):
        return pltpu.make_async_remote_copy(
            src_ref=gains.at[p],
            dst_ref=gains.at[p],
            send_sem=gain_s.at[k],
            recv_sem=gain_r.at[k],
            device_id=gx(k),
            device_id_type=MESH,
        )

    for k in range(1, n_gx):
        gain_copy(k).start()

    link_d, inverse_d, left_d, right_d = thirds_factors(X)
    inter_d = thirds_interface(n_gx, left_d, right_d)
    for x in range(X):
        units[0, x : x + 1, :] = jnp.full((1, C), left_d[x], f32)
        units[1, x : x + 1, :] = jnp.full((1, C), right_d[x], f32)

    each_received(lambda kind: goal_copy(kind).wait_recv())
    hits(1)
    hits(2)

    each_sent(lambda kind: halo_copy(kind).wait_send())
    each_received(lambda kind: halo_copy(kind).wait_recv())

    def arrived(kind):
        tiles = reps.at[kind, pl.ds(0 if kind else 1, n_yz if kind else n_yz - 1)]
        pltpu.make_async_remote_copy(
            src_ref=tiles,
            dst_ref=tiles,
            send_sem=rep_s.at[kind, 0],
            recv_sem=rep_r.at[kind],
            device_id=yz(1),
            device_id_type=MESH,
        ).wait_recv()

    arrived(0)

    each_received(arrived)
    for kind, (start, cells) in enumerate(((0, X), (X - HALO, HALO), (0, HALO))):
        sums = [None] * pack
        for k in range(n_yz):
            piece = answers[0] if kind == 0 and k == 0 else reps[kind, k]
            i = k % pack
            sums[i] = piece if sums[i] is None else sums[i] + piece
        total = sums[0]
        for i in range(1, pack):
            total = total + pltpu.roll(sums[i], GP - i * G, 1)
        goal_x = jnp.broadcast_to(goals[kind, 0:1, :], (ROWS, GP))
        stack = []
        for piece in split3(total):
            wide = piece.astype(f32)
            stack.append(
                jnp.concatenate(
                    [jnp.where(goal_x == x, wide, 0.0) for x in range(start, start + cells)],
                    axis=0,
                )
            )
        spread = jnp.dot(
            jnp.concatenate(stack, axis=1).astype(bf16),
            onehot_t[kind],
            preferred_element_type=f32,
        )
        base = (HALO, 0, HALO + X)[kind]
        for x in range(cells):
            fb[base + x] = fb[base + x] + spread[x * ROWS : (x + 1) * ROWS]

    yd, yg = ([], [])
    for x in range(X):
        at = HALO + x
        near, next2 = (fb[at + 1], fb[at + 2])
        back, back2 = (fb[at - 1], fb[at - 2])
        slope = (7.0 / 9.0 * inverse_d[x]) * (near - back) + (1.0 / 36.0 * inverse_d[x]) * (
            next2 - back2
        )
        smooth = coef[0, x] * fb[at] + coef[1, x] * (near + back) + coef[2, x] * (next2 + back2)
        for n in range(3, 6):
            smooth = smooth + coef[n, x] * (fb[at + n] + fb[at - n])
        if x:
            slope = slope - link_d[x] * yd[-1]
            smooth = smooth - coef[6, x] * yg[-1]
        yd.append(slope)
        yg.append(smooth)
    ud, ug = (yd[-1], yg[-1])
    last_d, last_g = (ud, ug)
    sol[0, X - 1] = ud
    sol[1, X - 1] = ug
    for x in range(X - 2, -1, -1):
        ud = yd[x] - link_d[x] * ud
        ug = yg[x] - coef[6, x] * ug
        sol[0, x] = ud
        sol[1, x] = ug
    here = edges.at[p]
    here[...] = jnp.zeros_like(here)
    for i, v in enumerate((ud, last_d, ug, last_g)):
        here[i * F : (i + 1) * F, :] = v[0:F]

    def edge_copy(k, rank, peer):
        return pltpu.make_async_remote_copy(
            src_ref=edges.at[rank],
            dst_ref=edges.at[rank],
            send_sem=edge_s.at[k],
            recv_sem=edge_r.at[k],
            device_id=peer,
            device_id_type=MESH,
        )

    for k in range(1, n_gx):
        edge_copy(k, p, gx(k)).start()

    for x in range(X):
        for f in range(F):
            out_d[f, x : x + 1, :] = sol[0, x, f : f + 1, :]
            out_g[f, x : x + 1, :] = sol[1, x, f : f + 1, :]

    inter_g = []
    gain = jnp.zeros((1, C), f32)
    for k in range(1, n_gx):
        gain_from(gains, gain_s, gain_r, k, p, r, n_gx).wait_recv()
    for q in range(n_gx):
        l0, l1 = (gains[q, 0:1, :], gains[q, 2:3, :])
        r0, r1 = (gains[q, 4:5, :], gains[q, 6:7, :])
        s = 1.0 / (1.0 - l0 * gain)
        gf = r0 * s
        ng = r1 + l1 * gain * gf
        inter_g.append((s, l0 * s, gf, l1, l1 * gain, ng))
        gain = ng

    for k in range(1, n_yz):
        req_copy(k).wait_send()
        rep_copy(0, k).wait_send()
    for k in range(1, n_gx):
        gain_copy(k).wait_send()

    def sent(kind):
        goal_copy(kind).wait_send()
        for k in range(n_yz):
            rep_copy(kind, k).wait_send()

    each_sent(sent)

    for k in range(1, n_gx):
        edge_copy(k, lax.rem(p - k + n_gx, n_gx), gx(-k)).wait_recv()

    for which, inter in enumerate((inter_d, inter_g)):
        hold = jnp.zeros((F, C), f32)
        first = []
        pick[which, 0, 0:F, :] = hold
        pick[which, 1, 0:1, :] = jnp.zeros((1, C), f32)
        for q in range(n_gx):
            s, ls, gf, l1, lg, ng = inter[q]
            h0 = edges[q, which * 2 * F : which * 2 * F + F, :]
            h1 = edges[q, which * 2 * F + F : which * 2 * F + 2 * F, :]
            hf = s * h0 + ls * hold
            hold = h1 + l1 * hold + lg * hf
            first.append(hf)
            pick[which, 3 * (q + 1), 0:F, :] = hold
            pick[which, 3 * (q + 1) + 1, 0:1, :] = jnp.broadcast_to(jnp.asarray(ng, f32), (1, C))
        after = jnp.zeros((F, C), f32)
        pick[which, 3 * n_gx + 2, 0:F, :] = after
        for q in range(n_gx - 1, -1, -1):
            after = first[q] + inter[q][2] * after
            pick[which, 3 * q + 2, 0:F, :] = after
        own_first = pick[which, 3 * p + 2, 0:F, :]
        before = pick[which, 3 * p, 0:F, :] + pick[which, 3 * p + 1, 0:1, :] * own_first
        before = jnp.where(p > 0, before, 0.0)
        after = pick[which, 3 * (p + 1) + 2, 0:F, :]
        ends[2 * which] = before
        ends[2 * which + 1] = after

    for k in range(1, n_gx):
        edge_copy(k, p, gx(k)).wait_send()


def gain_from(gains, gain_s, gain_r, k, p, r, n_gx):
    rank = lax.rem(p - k + n_gx, n_gx)
    return pltpu.make_async_remote_copy(
        src_ref=gains.at[rank],
        dst_ref=gains.at[rank],
        send_sem=gain_s.at[k],
        recv_sem=gain_r.at[k],
        device_id=(rank, r),
        device_id_type=MESH,
    )


def shards(fields, target, owner, sx, col, weights, sensor):
    F, X, C = fields.shape
    G = target.shape[1]
    n_gx, n_yz = (lax.axis_size("gx"), lax.axis_size("yz"))
    GP = max(G, 128)
    pack = GP // G
    edge_rows = -(-4 * F // ROWS) * ROWS
    f32, bf16 = (jnp.float32, jnp.bfloat16)
    vmem = pl.BlockSpec(memory_space=pltpu.VMEM)
    dma = pltpu.SemaphoreType.DMA
    hbm = pl.BlockSpec(memory_space=pltpu.HBM)
    inputs = (fields, target, target, sx, col, weights, sensor)
    out = pltpu.VMEM(fields.shape, f32)
    found = pl.pallas_call(
        functools.partial(kernel, n_gx, n_yz),
        out_shape=(out, out, pltpu.VMEM((4, X, C), f32), pltpu.VMEM((4, F, C), f32)),
        in_specs=[hbm] * 7,
        out_specs=(vmem, vmem, vmem, vmem),
        scratch_shapes=[
            *[pltpu.VMEM(a.shape, a.dtype) for a in inputs],
            dma((7,)),
            pltpu.VMEM((3 * F * X, C), bf16),
            pltpu.VMEM((3, 3 * GP, C), bf16),
            pltpu.VMEM((3, ROWS, GP), f32),
            pltpu.VMEM((n_yz, ROWS, GP), f32),
            pltpu.VMEM((3, n_yz, ROWS, GP), f32),
            pltpu.VMEM((n_yz // pack, ROWS, GP), f32),
            pltpu.VMEM((X + 2 * HALO, ROWS, C), f32),
            pltpu.VMEM((7, X, ROWS, C), f32),
            pltpu.VMEM((n_gx, ROWS, C), f32),
            pltpu.VMEM((n_gx, edge_rows, C), f32),
            pltpu.VMEM((2, X, ROWS, C), f32),
            pltpu.VMEM((2, 3 * (n_gx + 1), ROWS, C), f32),
            dma((n_yz,)),
            dma((n_yz,)),
            dma((3, n_yz)),
            dma((3,)),
            dma((3,)),
            dma((3,)),
            dma((n_gx,)),
            dma((n_gx,)),
            dma((3,)),
            dma((3,)),
            dma((n_gx,)),
            dma((n_gx,)),
        ],
        compiler_params=pltpu.CompilerParams(collective_id=0, has_side_effects=True),
    )(fields, target, owner.reshape(target.shape), sx, col, weights, sensor)
    own_d, own_g, units, ends = found

    def whole(local, i):
        low = ends[2 * i][:, None, :] * units[2 * i][None]
        return local + low + ends[2 * i + 1][:, None, :] * units[2 * i + 1][None]

    return (whole(own_d, 0), whole(own_g, 1))


def solution(mesh):
    placed = (
        P(None, "gx", "yz"),
        P("gx", "yz"),
        P("gx", "yz", None),
        P("gx", "yz"),
        P("gx", "yz"),
        P(None, "gx", "yz"),
        P("gx", "yz"),
    )
    return jax.shard_map(
        shards,
        mesh=mesh,
        in_specs=placed,
        out_specs=(P(None, "gx", "yz"), P(None, "gx", "yz")),
        check_vma=False,
    )
```
